768 devices in a mesh: space: 192 (over x_lo, z, y), tracer: 4 (over x_hi, core).
Axes of the slice: x: 4 (x_hi: 2, x_lo: 2; x = x_hi * 2 + x_lo), y: 8, z: 12, core: 2. Of those that a mesh axis runs over, the one named last changes fastest.
Arguments:
- populations: float32 [19, 1536, 16, 128], P(None, 'space', 'tracer'), may hold values from 0 to 0.5
- solid_mask: int32 [1536, 16, 128], P('space', 'tracer'), may hold values 0 or 1
- tracers: float32 [64, 1536, 16, 128], P('tracer', 'space'), may hold values from 0.05 to 2
- decay_rates: float32 [64], P('tracer'), may hold values from 0.02 to 0.4
- buoyancy_coeffs: float32 [64], P('tracer'), may hold values from -0.04 to 0.04
- source_cells: int32 [64, 8], P('tracer'), may hold values from 0 to 3145727
- source_rates: float32 [64, 8], P('tracer'), may hold values from 0.5 to 4
Outputs:
- populations_out: float32 [19, 1536, 16, 128], P(None, 'space', 'tracer')
- velocity_out: float32 [3, 1536, 16, 128], P(None, 'space', 'tracer')
- tracers_out: float32 [64, 1536, 16, 128], P('tracer', 'space')
The draws below stay inside these ranges and needn't reach their ends.
All inputs are finite; a program needn't handle non-finite values. No bound on the sum of `solid_mask` on one device may be relied on, other than what follows from the above.
Results may differ from the reference program's by a relative error of at most 0.0003.
Values may be sent and summed in bfloat16 or wider, within the bound.
A program may use at most 32 MiB of HBM per device.

```python
import math
import jax
import jax.numpy as jnp
from jax import lax

NY = 16
NZ = 128
TRACERS = 64
SOURCES = 8
SECTIONS = 2
NX = 1536


lattice_dirs = ((0, 0, 0), (1, 0, 0), (-1, 0, 0), (0, 1, 0), (0, -1, 0), (0, 0, 1), (0, 0, -1), (1, 1, 0), (-1, -1, 0), (1, -1, 0), (-1, 1, 0), (1, 0, 1), (-1, 0, -1), (1, 0, -1), (-1, 0, 1), (0, 1, 1), (0, -1, -1), (0, 1, -1), (0, -1, 1))


lattice_weights = (1.0 / 3.0,) + (1.0 / 18.0,) * 6 + (1.0 / 36.0,) * 12


def draw_populations(key, part):
    keys = jax.random.split(jax.random.fold_in(key, 7), 3)
    density = jax.random.uniform(keys[0], (NX, NY, NZ), jnp.float32, 0.9, 1.1)
    velocity = jnp.clip(0.05 * jax.random.normal(keys[1], (3, NX, NY, NZ), jnp.float32), -0.15, 0.15)
    noise = jax.random.uniform(keys[2], (19, NX, NY, NZ), jnp.float32, -0.1, 0.1)
    speed_sq = velocity[0] * velocity[0] + velocity[1] * velocity[1] + velocity[2] * velocity[2]
    equals = []
    for direction in range(19):
        offsets = lattice_dirs[direction]
        along = offsets[0] * velocity[0] + offsets[1] * velocity[1] + offsets[2] * velocity[2]
        equals.append(lattice_weights[direction] * density * (1.0 + 3.0 * along + 4.5 * along * along - 1.5 * speed_sq))
    return jnp.stack(equals) * (1.0 + noise)


def place_ends(values, own_key, smallest, high):
    dims = values.shape
    spot = [jax.random.randint(jax.random.fold_in(own_key, axis), (), 0, dims[axis]) for axis in range(len(dims))]
    values = values.at[tuple(spot)].set(smallest)
    longest = dims.index(max(dims))
    spot[longest] = (spot[longest] + 1) % dims[longest]
    return values.at[tuple(spot)].set(high)


def steps_of(rng, extent, shards, smallest, largest):
    level, own = 1.0, jax.random.fold_in(rng, 6)
    for position, parts in shards:
        steps = jnp.exp(jax.random.uniform(jax.random.fold_in(own, position), (parts,), jnp.float32, smallest / len(shards), largest / len(shards)))
        level = level * jnp.repeat(steps, extent[position] // parts).reshape([-1 if axis == position else 1 for axis in range(len(extent))])
    return level


def setup_inputs(seed: int = 0) -> dict:
    key_of = jax.random.split(jax.random.key(seed), 8)
    populations = draw_populations(jax.random.fold_in(key_of[7], 71), 0)
    solid_mask = place_ends((jax.random.randint(key_of[1], (NX, NY, NZ), 0, 6) < 1).astype(jnp.int32), jax.random.fold_in(key_of[1], 1), 0, 1)
    tracers = jnp.clip(jnp.exp(math.log(2.0) - 3.6888794 * jax.random.uniform(key_of[2], (TRACERS, NX, NY, NZ), jnp.float32) ** steps_of(key_of[2], (TRACERS, NX, NY, NZ), ((0, 4), (1, 192)), -0.2, 0.2)), 0.05, 2.0)
    decay_rates = jnp.clip(jnp.exp(math.log(0.4) - 2.9957323 * jax.random.uniform(key_of[3], (TRACERS,), jnp.float32) ** steps_of(key_of[3], (TRACERS,), ((0, 4),), -0.2, 0.2)), 0.02, 0.4)
    buoyancy_coeffs = jnp.clip(jax.random.uniform(key_of[4], (TRACERS,), jnp.float32, -0.04, 0.04) * steps_of(key_of[4], (TRACERS,), ((0, 4),), -0.4, 0.0), -0.04, 0.04)
    source_cells = place_ends(jax.random.randint(key_of[5], (TRACERS, SOURCES), 0, NX * NY * NZ), jax.random.fold_in(key_of[5], 1), 0, (NX * NY * NZ) - 1).astype(jnp.int32)
    source_rates = jnp.clip(jnp.exp(math.log(4.0) - 2.0794415 * jax.random.uniform(key_of[6], (TRACERS, SOURCES), jnp.float32) ** steps_of(key_of[6], (TRACERS, SOURCES), ((0, 4),), -0.2, 0.2)), 0.5, 4.0)
    return dict(populations=populations, solid_mask=solid_mask, tracers=tracers, decay_rates=decay_rates, buoyancy_coeffs=buoyancy_coeffs, source_cells=source_cells, source_rates=source_rates)


lattice_dirs = ((0, 0, 0), (1, 0, 0), (-1, 0, 0), (0, 1, 0), (0, -1, 0), (0, 0, 1), (0, 0, -1),
                (1, 1, 0), (-1, -1, 0), (1, -1, 0), (-1, 1, 0), (1, 0, 1), (-1, 0, -1),
                (1, 0, -1), (-1, 0, 1), (0, 1, 1), (0, -1, -1), (0, 1, -1), (0, -1, 1))
lattice_weights = (1.0 / 3.0,) + (1.0 / 18.0,) * 6 + (1.0 / 36.0,) * 12
opposite = (0, 2, 1, 4, 3, 6, 5, 8, 7, 10, 9, 12, 11, 14, 13, 16, 15, 18, 17)
relax_rate = 1.25


def moments(lattice):
    density = jnp.sum(lattice, axis=0)
    velocity_parts = []
    for axis_num in range(3):
        total = jnp.zeros_like(density)
        for direction in range(19):
            component = lattice_dirs[direction][axis_num]
            if component != 0:
                total = total + component * lattice[direction]
        velocity_parts.append(total / density)
    return density, jnp.stack(velocity_parts)


def collide(lattice, force):
    density, velocity = moments(lattice)
    speed_sq = velocity[0] * velocity[0] + velocity[1] * velocity[1] + velocity[2] * velocity[2]
    posts = []
    for direction in range(19):
        offsets = lattice_dirs[direction]
        weight = lattice_weights[direction]
        along = offsets[0] * velocity[0] + offsets[1] * velocity[1] + offsets[2] * velocity[2]
        equal = weight * density * (1.0 + 3.0 * along + 4.5 * along * along - 1.5 * speed_sq)
        posts.append(lattice[direction] - relax_rate * (lattice[direction] - equal) + 3.0 * weight * offsets[2] * force)
    return jnp.stack(posts)


def stream(padded, post, fluid):
    span_x, span_y, span_z = post.shape[1], post.shape[2], post.shape[3]
    fresh = []
    for direction in range(19):
        offsets = lattice_dirs[direction]
        low_x, low_y, low_z = 1 - offsets[0], 1 - offsets[1], 1 - offsets[2]
        neighbour = padded[direction, low_x:low_x + span_x, low_y:low_y + span_y, low_z:low_z + span_z]
        open_side = padded[19, low_x:low_x + span_x, low_y:low_y + span_y, low_z:low_z + span_z]
        bounced = post[opposite[direction]]
        fresh.append(fluid * (open_side * neighbour + (1.0 - open_side) * bounced) + (1.0 - fluid) * post[direction])
    return jnp.stack(fresh)


def lattice_step(lattice, fluid, force):
    post = collide(lattice, force)
    payload = jnp.concatenate([post, fluid[None]], axis=0)
    padded = jnp.pad(payload, ((0, 0), (1, 1), (1, 1), (1, 1)))
    return stream(padded, post, fluid)


def window(array, axis_num, start, count):
    return lax.slice_in_dim(array, start, start + count, axis=axis_num)


def minmod(first, second):
    return 0.5 * (jnp.sign(first) + jnp.sign(second)) * jnp.minimum(jnp.abs(first), jnp.abs(second))


def face_flux(conc, speed, fluid, axis_num):
    count = conc.shape[axis_num] - 4
    behind = window(conc, axis_num, 0, count + 1)
    current = window(conc, axis_num, 1, count + 1)
    ahead_one = window(conc, axis_num, 2, count + 1)
    ahead_two = window(conc, axis_num, 3, count + 1)
    left_state = current + 0.5 * minmod(current - behind, ahead_one - current)
    right_state = ahead_one - 0.5 * minmod(ahead_one - current, ahead_two - ahead_one)
    face_speed = 0.5 * (window(speed, axis_num, 1, count + 1) + window(speed, axis_num, 2, count + 1))
    face_speed = face_speed * window(fluid, axis_num, 1, count + 1) * window(fluid, axis_num, 2, count + 1)
    flux = jnp.maximum(face_speed, 0.0) * left_state + jnp.minimum(face_speed, 0.0) * right_state
    return window(flux, axis_num, 1, count) - window(flux, axis_num, 0, count)


def tracer_section(conc, flow, rates, emission):
    count = conc.shape[1] - 4

    def inner(array):
        return window(array, 1, 2, count)

    def pad_side(array, axis_num):
        widths = [(0, 0)] * 4
        widths[axis_num] = (2, 2)
        return jnp.pad(array, widths)

    air = flow[3:4]
    div_x = face_flux(conc, flow[0:1], air, 1)
    div_y = face_flux(pad_side(inner(conc), 2), pad_side(inner(flow[1:2]), 2), pad_side(inner(air), 2), 2)
    div_z = face_flux(pad_side(inner(conc), 3), pad_side(inner(flow[2:3]), 3), pad_side(inner(air), 3), 3)
    center = inner(conc)
    rate_col = rates[:, None, None, None]
    lost = rate_col * center
    paired = lost.reshape((lost.shape[0] // 2, 2) + lost.shape[1:])
    produced = jnp.stack([jnp.zeros_like(paired[:, 0]), paired[:, 0]], axis=1).reshape(center.shape)
    return center + (produced - lost - (div_x + div_y + div_z) + emission)


def reference(populations, solid_mask, tracers, decay_rates, buoyancy_coeffs, source_cells, source_rates):
    fluid = 1.0 - solid_mask.astype(jnp.float32)
    lattice = populations
    for turn in range(2):
        lattice = lattice_step(lattice, fluid, 0.0)
    density, velocity = moments(lattice)
    flow_half = jnp.concatenate([velocity * fluid, fluid[None]], axis=0).astype(jnp.bfloat16)
    flow = lax.optimization_barrier(flow_half).astype(jnp.float32)
    flow_pad = jnp.pad(flow, ((0, 0), (2, 2), (0, 0), (0, 0)))

    def advance(items):
        tracer_pair, pair_rates, pair_cells, strengths = items
        rows = jnp.arange(2).astype(jnp.int32)[:, None]
        emission = jnp.zeros((2, NX * NY * NZ), jnp.float32).at[rows, pair_cells.astype(jnp.int32)].add(strengths)
        emission = emission.reshape(2, NX, NY, NZ)
        for section in range(SECTIONS):
            tracer_pair = tracer_section(jnp.pad(tracer_pair, ((0, 0), (2, 2), (0, 0), (0, 0))), flow_pad, pair_rates, emission)
        return tracer_pair

    conc = lax.map(advance, (tracers.reshape(TRACERS // 2, 2, NX, NY, NZ), decay_rates.reshape(TRACERS // 2, 2),
                             source_cells.reshape(TRACERS // 2, 2, SOURCES), source_rates.reshape(TRACERS // 2, 2, SOURCES)))
    conc = conc.reshape(TRACERS, NX, NY, NZ)
    buoyancy = jnp.einsum("t,txyz->xyz", buoyancy_coeffs, conc, precision=lax.Precision.HIGHEST)
    lattice = lattice_step(lattice, fluid, buoyancy)
    density, velocity = moments(lattice)
    return lattice, velocity * fluid, conc
```

```python
import functools

import jax
import jax.numpy as jnp
from jax import lax
from jax.experimental import pallas as pl
from jax.experimental.pallas import tpu as pltpu
from jax.sharding import PartitionSpec as P

DIRS = (
    (0, 0, 0),
    (1, 0, 0),
    (-1, 0, 0),
    (0, 1, 0),
    (0, -1, 0),
    (0, 0, 1),
    (0, 0, -1),
    (1, 1, 0),
    (-1, -1, 0),
    (1, -1, 0),
    (-1, 1, 0),
    (1, 0, 1),
    (-1, 0, -1),
    (1, 0, -1),
    (-1, 0, 1),
    (0, 1, 1),
    (0, -1, -1),
    (0, 1, -1),
    (0, -1, 1),
)
WEIGHTS = (1.0 / 3.0,) + (1.0 / 18.0,) * 6 + (1.0 / 36.0,) * 12
OPP = (0, 2, 1, 4, 3, 6, 5, 8, 7, 10, 9, 12, 11, 14, 13, 16, 15, 18, 17)
RELAX = 1.25
XD = ((1, 7, 9, 11, 13), (2, 8, 10, 12, 14))
YD = ((3, 7, 10, 15, 17), (4, 8, 9, 16, 18))
CORNERS = ((7, -1, -1), (9, -1, 1), (10, 1, -1), (8, 1, 1))
CORNER_OF = {7: 0, 9: 1, 10: 2, 8: 3}
FLAG = 5
SX, NY, NZ = 8, 16, 128
TY = 4
CHUNKS = 4
F32 = jnp.float32


def kernel(
    n_space,
    n_tracer,
    decay_ref,
    coeff_ref,
    cells_ref,
    rates_ref,
    pop_hbm,
    mask_hbm,
    tracer_hbm,
    pop_out,
    vel_out,
    tracer_out,
    fin,
    mask_in,
    fluid_v,
    both,
    post,
    xs,
    xr,
    ys,
    yr,
    cs,
    cr,
    flow_f,
    fb,
    gflow,
    face_x,
    face_y,
    face_z,
    cext,
    csec,
    cout,
    emis,
    part,
    sb,
    rb,
    rx,
    fout,
    vout,
    load_sem,
    out_sem,
    halo_send,
    halo_recv,
    bulk_send,
    bulk_recv,
    flow_send,
    flow_recv,
    buoy_send,
    buoy_recv,
):
    sp = lax.axis_index("space")
    tr = lax.axis_index("tracer")
    space = {-1: lax.rem(sp + n_space - 1, n_space), 0: sp, 1: lax.rem(sp + 1, n_space)}
    trs = [lax.rem(tr + k, n_tracer) for k in range(n_tracer)]
    group = tracer_hbm.shape[0]
    piece = group // CHUNKS

    def rcopy(src, dst, ssem, rsem, ds, t):
        return pltpu.make_async_remote_copy(
            src_ref=src,
            dst_ref=dst,
            send_sem=ssem,
            recv_sem=rsem,
            device_id=(space[ds], t),
            device_id_type=pl.DeviceIdType.MESH,
        )

    load_pop = pltpu.make_async_copy(pop_hbm, fin, load_sem.at[0])
    load_mask = pltpu.make_async_copy(mask_hbm, mask_in, load_sem.at[1])
    load_tracer = pltpu.make_async_copy(tracer_hbm, cext.at[:, 4 : 4 + SX], load_sem.at[2])
    load_pop.start()
    load_mask.start()
    load_tracer.start()

    barrier = pltpu.get_barrier_semaphore()
    peers = [(ds, k) for ds in (-1, 0, 1) for k in range(n_tracer) if (ds, k) != (0, 0)]
    for ds, k in peers:
        pl.semaphore_signal(
            barrier, inc=1, device_id=(space[ds], trs[k]), device_id_type=pl.DeviceIdType.MESH
        )

    xi = lax.broadcasted_iota(jnp.int32, (SX, NZ), 0)
    zi = lax.broadcasted_iota(jnp.int32, (SX, NZ), 1)

    def moments(f):
        even = {}
        rho = f[0]
        u = [None, None, None]
        for q in range(1, 19, 2):
            rho = rho + (f[q] + f[q + 1])
            diff = f[q] - f[q + 1]
            for a in range(3):
                e = DIRS[q][a]
                if e == 1:
                    u[a] = diff if u[a] is None else u[a] + diff
                elif e == -1:
                    u[a] = -diff if u[a] is None else u[a] - diff
        inv = 1.0 / rho
        return rho, [v * inv for v in u]

    def collide(f, rho, u):
        base = 1.0 - 1.5 * (u[0] * u[0] + u[1] * u[1] + u[2] * u[2])
        scaled = RELAX * rho
        out = [None] * 19
        out[0] = (1.0 - RELAX) * f[0] + (WEIGHTS[0] * scaled) * base
        for q in range(1, 19, 2):
            along = None
            for a in range(3):
                e = DIRS[q][a]
                if e == 1:
                    along = u[a] if along is None else along + u[a]
                elif e == -1:
                    along = -u[a] if along is None else along - u[a]
            wr = WEIGHTS[q] * scaled
            sym = wr * (base + 4.5 * along * along)
            asym = wr * (3.0 * along)
            out[q] = (1.0 - RELAX) * f[q] + (sym + asym)
            out[q + 1] = (1.0 - RELAX) * f[q + 1] + (sym - asym)
        return out

    def keep_post(step, y, p):
        buf = step % 2
        for q in range(19):
            post[buf, q, y] = p[q]
        for k in range(5):
            xs[step, 0, k, y : y + 1, :] = p[XD[1][k]][0:1, :]
            xs[step, 1, k, y : y + 1, :] = p[XD[0][k]][SX - 1 : SX, :]
            if y == 0:
                ys[step, 0, k] = p[YD[1][k]]
            if y == TY - 1:
                ys[step, 1, k] = p[YD[0][k]]
        for c, (q, dx, dy) in enumerate(CORNERS):
            if y == (TY - 1 if dy < 0 else 0):
                row = p[q][SX - 1 : SX, :] if dx < 0 else p[q][0:1, :]
                cs[step, c, 0] = jnp.broadcast_to(row, (SX, NZ))

    def messages(step):
        n = 6 if step == 0 else 5
        part_of = pl.ds(0, n)
        m = 2 if step == 0 else 1
        out = []
        out.append((xs.at[step, 1, part_of], xr.at[step, 0, part_of], 1, 0))
        out.append((xs.at[step, 0, part_of], xr.at[step, 1, part_of], -1, 0))
        out.append((ys.at[step, 1, part_of], yr.at[step, 0, part_of], 0, 1))
        out.append((ys.at[step, 0, part_of], yr.at[step, 1, part_of], 0, n_tracer - 1))
        for c, (q, dx, dy) in enumerate(CORNERS):
            out.append(
                (
                    cs.at[step, c, pl.ds(0, m)],
                    cr.at[step, c, pl.ds(0, m)],
                    -dx,
                    1 if dy < 0 else n_tracer - 1,
                )
            )
        return [
            rcopy(s, d, halo_send.at[step, i], halo_recv.at[step, i], ds, trs[k])
            for i, (s, d, ds, k) in enumerate(out)
        ]

    def bulk(j):
        rows = pl.ds(j * piece, piece)
        return (
            rcopy(
                tracer_hbm.at[rows, pl.ds(SX - 4, 4)],
                cext.at[rows, pl.ds(0, 4)],
                bulk_send.at[0, j],
                bulk_recv.at[0, j],
                1,
                tr,
            ),
            rcopy(
                tracer_hbm.at[rows, pl.ds(0, 4)],
                cext.at[rows, pl.ds(SX + 4, 4)],
                bulk_send.at[1, j],
                bulk_recv.at[1, j],
                -1,
                tr,
            ),
        )

    def shifted(step, buf, q, y):
        ex, ey, ez = DIRS[q]
        yy = y - ey
        if yy < 0:
            v = yr[step, 0, YD[0].index(q)]
        elif yy >= TY:
            v = yr[step, 1, YD[1].index(q)]
        else:
            v = post[buf, q, yy]
        if ex != 0:
            side = 0 if ex == 1 else 1
            if 0 <= yy < TY:
                row = xr[step, side, XD[side].index(q), yy : yy + 1, :]
            else:
                row = cr[step, CORNER_OF[q], 0, 0:1, :]
            v = pltpu.roll(v, 1 if ex == 1 else SX - 1, 0)
            v = jnp.where(xi == (0 if ex == 1 else SX - 1), row, v)
        if ez != 0:
            v = pltpu.roll(v, 1 if ez == 1 else NZ - 1, 1)
        return v

    def stream(step, y):
        buf = step % 2
        air = fluid_v[y] > 0.5
        here = [post[buf, q, y] for q in range(19)]
        fresh = [here[0]]
        for q in range(1, 19):
            back = jnp.where(air, here[OPP[q]], here[q])
            fresh.append(jnp.where(both[q, y] > 0.5, shifted(step, buf, q, y), back))
        return fresh

    load_mask.wait()
    for y in range(TY):
        m = mask_in[pl.ds(y, SX, stride=TY), :]
        air = 1.0 - m.astype(F32)
        fluid_v[y] = air
        for side, x in ((0, 0), (1, SX - 1)):
            xs[0, side, FLAG, y : y + 1, :] = air[x : x + 1, :]
        if y == 0:
            ys[0, 0, FLAG] = air
        if y == TY - 1:
            ys[0, 1, FLAG] = air
        for c, (q, dx, dy) in enumerate(CORNERS):
            if y == (TY - 1 if dy < 0 else 0):
                row = air[SX - 1 : SX, :] if dx < 0 else air[0:1, :]
                cs[0, c, 1] = jnp.broadcast_to(row, (SX, NZ))
    load_pop.wait()
    for y in range(TY):
        f = [fin[pl.ds(q * SX * TY + y, SX, stride=TY), :] for q in range(19)]
        rho, u = moments(f)
        keep_post(0, y, collide(f, rho, u))

    pl.semaphore_wait(barrier, len(peers))
    first = messages(0)
    for c in first:
        c.start()
    sent_bulk = [bulk(j) for j in range(CHUNKS)]
    for c in sent_bulk[0]:
        c.start()

    yi16 = lax.broadcasted_iota(jnp.int32, (NY, NZ), 0)
    zi16 = lax.broadcasted_iota(jnp.int32, (NY, NZ), 1)
    flat = yi16 * NZ + zi16
    origin = (sp * SX - 2) * (NY * NZ)

    def emit(t, carry):
        for r in range(SX + 4):
            total = jnp.zeros((NY, NZ), F32)
            for s in range(cells_ref.shape[0]):
                key = cells_ref[s, t] - (origin + r * NY * NZ)
                total = total + jnp.where(flat == key, rates_ref[s, t], 0.0)
            emis[t, r] = total
        return carry

    lax.fori_loop(0, group, emit, 0)

    for c in first:
        c.wait_recv()

    has_x = (
        jnp.where(sp > 0, 1.0, 0.0).astype(F32),
        jnp.where(sp < n_space - 1, 1.0, 0.0).astype(F32),
    )
    has_y = (
        jnp.where(tr > 0, 1.0, 0.0).astype(F32),
        jnp.where(tr < n_tracer - 1, 1.0, 0.0).astype(F32),
    )
    for y in range(TY):
        mine = fluid_v[y]
        for q in range(1, 19):
            ex, ey, ez = DIRS[q]
            yy = y - ey
            if yy < 0:
                v = yr[0, 0, FLAG] * has_y[0]
            elif yy >= TY:
                v = yr[0, 1, FLAG] * has_y[1]
            else:
                v = fluid_v[yy]
            if ex != 0:
                side = 0 if ex == 1 else 1
                if 0 <= yy < TY:
                    row = xr[0, side, FLAG, yy : yy + 1, :] * has_x[side]
                else:
                    row = cr[0, CORNER_OF[q], 1, 0:1, :] * (has_x[side] * has_y[0 if yy < 0 else 1])
                v = pltpu.roll(v, 1 if ex == 1 else SX - 1, 0)
                v = jnp.where(xi == (0 if ex == 1 else SX - 1), row, v)
            if ez != 0:
                v = pltpu.roll(v, 1 if ez == 1 else NZ - 1, 1)
                v = jnp.where(zi == (0 if ez == 1 else NZ - 1), 0.0, v)
            both[q, y] = v * mine

    for y in range(TY):
        f = stream(0, y)
        rho, u = moments(f)
        keep_post(1, y, collide(f, rho, u))
    second = messages(1)
    for c in second:
        c.start()
    for c in sent_bulk[1]:
        c.start()
    for c in second:
        c.wait_recv()

    for y in range(TY):
        f = stream(1, y)
        rho, u = moments(f)
        air = fluid_v[y]
        for a in range(3):
            flow_f[pl.ds(a * TY + y, SX, stride=4 * TY), :] = u[a] * air
        flow_f[pl.ds(3 * TY + y, SX, stride=4 * TY), :] = air
        keep_post(2, y, collide(f, rho, u))
    for x in range(SX):
        fb[tr, 3 + x] = flow_f[x * 4 * TY : (x + 1) * 4 * TY, :].astype(jnp.bfloat16)

    def flow_messages():
        out = []
        for ds in (0, 1, -1):
            for k in range(n_tracer):
                if (ds, k) == (0, 0):
                    continue
                if ds == 0:
                    src, dst, kind = pl.ds(3, SX), pl.ds(3, SX), 0
                elif ds == 1:
                    src, dst, kind = pl.ds(SX, 3), pl.ds(0, 3), 1
                else:
                    src, dst, kind = pl.ds(3, 3), pl.ds(SX + 3, 3), 2
                out.append(
                    rcopy(
                        fb.at[tr, src],
                        fb.at[tr, dst],
                        flow_send.at[kind, k],
                        flow_recv.at[kind, tr],
                        ds,
                        trs[k],
                    )
                )
        return out

    def flow_arrivals():
        out = []
        for kind, rows in ((0, pl.ds(3, SX)), (1, pl.ds(0, 3)), (2, pl.ds(SX + 3, 3))):
            for k in range(n_tracer):
                if (kind, k) == (0, 0):
                    continue
                t = trs[k]
                out.append(
                    rcopy(
                        fb.at[t, rows],
                        fb.at[t, rows],
                        flow_send.at[kind, k],
                        flow_recv.at[kind, t],
                        1,
                        t,
                    )
                )
        return out

    flows = flow_messages()
    for c in flows:
        c.start()
    third = messages(2)
    for c in third:
        c.start()
    for j in range(2, CHUNKS):
        for c in sent_bulk[j]:
            c.start()
    load_tracer.wait()
    for c in flow_arrivals():
        c.wait_recv()

    def widen(x, carry):
        for t in range(n_tracer):
            v = fb[t, x].astype(F32)
            for a in range(4):
                gflow[a, x, t * TY : (t + 1) * TY, :] = v[a * TY : (a + 1) * TY, :]
        return carry

    lax.fori_loop(0, SX + 6, widen, 0)

    @pl.when(sp == 0)
    def _():
        for x in range(3):
            gflow[3, x] = jnp.zeros((NY, NZ), F32)

    @pl.when(sp == n_space - 1)
    def _():
        for x in range(SX + 3, SX + 6):
            gflow[3, x] = jnp.zeros((NY, NZ), F32)

    def split(ref, i, s):
        ref[0, i] = jnp.maximum(s, 0.0)
        ref[1, i] = jnp.minimum(s, 0.0)

    def faces_x(i, carry):
        split(
            face_x,
            i,
            0.5 * (gflow[0, i] + gflow[0, i + 1]) * gflow[3, i] * gflow[3, i + 1],
        )
        return carry

    lax.fori_loop(0, SX + 5, faces_x, 0)

    def faces_yz(i, carry):
        air = gflow[3, i + 1]
        v = gflow[1, i + 1]
        s = 0.5 * (v + pltpu.roll(v, NY - 1, 0)) * air * pltpu.roll(air, NY - 1, 0)
        split(face_y, i, jnp.where(yi16 == NY - 1, 0.0, s))
        v = gflow[2, i + 1]
        s = 0.5 * (v + pltpu.roll(v, NZ - 1, 1)) * air * pltpu.roll(air, NZ - 1, 1)
        split(face_z, i, jnp.where(zi16 == NZ - 1, 0.0, s))
        return carry

    lax.fori_loop(0, SX + 4, faces_yz, 0)

    def limited(below, above):
        return 0.5 * jnp.minimum(
            jnp.maximum(below, jnp.minimum(above, 0.0)), jnp.maximum(above, 0.0)
        )

    def along_axis(c, axis, size, index, up, down):
        above = jnp.where(index == size - 1, 0.0, pltpu.roll(c, size - 1, axis)) - c
        below = c - jnp.where(index == 0, 0.0, pltpu.roll(c, 1, axis))
        h = limited(below, above)
        flux = up * (c + h) + down * pltpu.roll(c - h, size - 1, axis)
        return flux - pltpu.roll(flux, 1, axis)

    def section(src, t, rows, face_shift, yz_shift, emit_shift, store):
        rate = decay_ref[t]
        before = jnp.maximum(t - 1, 0)
        gain = jnp.where(lax.rem(t, 2) == 1, decay_ref[before], 0.0)
        below = src[t, 1] - src[t, 0]
        flux_low = None
        left_low = None
        for j in range(1, rows + 3):
            c = src[t, j]
            above = src[t, j + 1] - c
            h = limited(below, above)
            if j >= 2:
                f = j - 1 + face_shift
                flux = face_x[0, f] * left_low + face_x[1, f] * (c - h)
                if j >= 3:
                    r = j - 3
                    mid = src[t, j - 1]
                    div = flux - flux_low
                    i = r + yz_shift
                    div = div + along_axis(mid, 0, NY, yi16, face_y[0, i], face_y[1, i])
                    div = div + along_axis(mid, 1, NZ, zi16, face_z[0, i], face_z[1, i])
                    made = gain * src[before, j - 1] - rate * mid
                    store(r, mid + (made - div + emis[t, r + emit_shift]))
                flux_low = flux
            left_low = c + h
            below = above

    def section_one(j, carry):
        for c in bulk(j):
            c.wait_recv()

        def clear(rows):
            def body(t, carry):
                for x in rows:
                    cext[j * piece + t, x] = jnp.zeros((NY, NZ), F32)
                return carry

            lax.fori_loop(0, piece, body, 0)

        @pl.when(sp == 0)
        def _():
            clear(range(4))

        @pl.when(sp == n_space - 1)
        def _():
            clear(range(SX + 4, SX + 8))

        def one(i, carry):
            t = j * piece + i

            def store(r, v):
                csec[t, r] = v

            section(cext, t, SX + 4, -1, 0, 0, store)
            return carry

        return lax.fori_loop(0, piece, one, carry)

    lax.fori_loop(0, CHUNKS, section_one, 0)

    for x in range(SX):
        part[x] = jnp.zeros((NY, NZ), F32)

    def section_two(t, carry):
        weight = coeff_ref[t]

        def store(r, v):
            cout[t, r] = v
            part[r] = part[r] + weight * v

        section(csec, t, SX, 1, 2, 2, store)
        return carry

    lax.fori_loop(0, group, section_two, 0)
    save_tracer = pltpu.make_async_copy(cout, tracer_out, out_sem.at[0])
    save_tracer.start()

    for x in range(SX):
        v = part[x]
        for t in range(n_tracer):
            sb[t, x * 8 : (x + 1) * 8, :] = pltpu.roll(v, (1 - TY * t) % NY, 0)[0:8]
    buoy = []
    for ds, rows, dst in ((1, pl.ds((SX - 1) * 8, 8), 0), (-1, pl.ds(0, 8), 1)):
        for k in range(n_tracer):
            buoy.append(
                rcopy(
                    sb.at[trs[k], rows],
                    rx.at[dst, k],
                    buoy_send.at[dst + 1, k],
                    buoy_recv.at[dst + 1, k],
                    ds,
                    trs[k],
                )
            )
    for k in range(1, n_tracer):
        buoy.append(
            rcopy(sb.at[trs[k]], rb.at[k], buoy_send.at[0, k], buoy_recv.at[0, k], 0, trs[k])
        )
    for c in buoy:
        c.start()
    for c in third:
        c.wait_recv()
    for c in buoy:
        c.wait_recv()

    buf = 0
    for yy in range(-1, TY + 1):
        g = sb[tr, pl.ds(yy + 1, SX, stride=8), :]
        for k in range(1, n_tracer):
            g = g + rb[k, pl.ds(yy + 1, SX, stride=8), :]
        if yy < 0 or yy >= TY:
            side = 0 if yy < 0 else 1
            for k, q in enumerate(YD[side]):
                if DIRS[q][2]:
                    yr[2, side, k] = yr[2, side, k] + (3.0 * WEIGHTS[q] * DIRS[q][2]) * g
        else:
            for q in range(19):
                if DIRS[q][2]:
                    post[buf, q, yy] = post[buf, q, yy] + (3.0 * WEIGHTS[q] * DIRS[q][2]) * g
    for side in range(2):
        g = rx[side, 0]
        for k in range(1, n_tracer):
            g = g + rx[side, k]
        g = pltpu.roll(g, 7, 0)
        for k, q in enumerate(XD[side]):
            if DIRS[q][2]:
                xr[2, side, k] = xr[2, side, k] + (3.0 * WEIGHTS[q] * DIRS[q][2]) * g

    for y in range(TY):
        f = stream(2, y)
        rho, u = moments(f)
        for q in range(19):
            fout[pl.ds(q * SX * TY + y, SX, stride=TY), :] = f[q]
        for a in range(3):
            vout[pl.ds(a * SX * TY + y, SX, stride=TY), :] = u[a] * fluid_v[y]
    save_pop = pltpu.make_async_copy(fout, pop_out, out_sem.at[1])
    save_vel = pltpu.make_async_copy(vout, vel_out, out_sem.at[2])
    save_pop.start()
    save_vel.start()

    for c in first + second + third + flows + buoy:
        c.wait_send()
    for pair in sent_bulk:
        for c in pair:
            c.wait_send()
    save_tracer.wait()
    save_pop.wait()
    save_vel.wait()


def local(
    n_space,
    n_tracer,
    populations,
    solid_mask,
    tracers,
    decay_rates,
    buoyancy_coeffs,
    source_cells,
    source_rates,
):
    group = tracers.shape[0]
    rows = SX * TY
    smem = pl.BlockSpec(memory_space=pltpu.SMEM)
    hbm = pl.BlockSpec(memory_space=pl.ANY)
    vmem = pltpu.VMEM
    dma = pltpu.SemaphoreType.DMA
    out = pl.pallas_call(
        functools.partial(kernel, n_space, n_tracer),
        out_shape=(
            jax.ShapeDtypeStruct((19 * rows, NZ), F32),
            jax.ShapeDtypeStruct((3 * rows, NZ), F32),
            jax.ShapeDtypeStruct(tracers.shape, F32),
        ),
        in_specs=[smem] * 4 + [hbm] * 3,
        out_specs=(hbm, hbm, hbm),
        scratch_shapes=[
            vmem((19 * rows, NZ), F32),
            vmem((rows, NZ), jnp.int32),
            vmem((TY, SX, NZ), F32),
            vmem((19, TY, SX, NZ), F32),
            vmem((2, 19, TY, SX, NZ), F32),
            vmem((3, 2, 6, 8, NZ), F32),
            vmem((3, 2, 6, 8, NZ), F32),
            vmem((3, 2, 6, 8, NZ), F32),
            vmem((3, 2, 6, 8, NZ), F32),
            vmem((3, 4, 2, 8, NZ), F32),
            vmem((3, 4, 2, 8, NZ), F32),
            vmem((SX * 4 * TY, NZ), F32),
            vmem((n_tracer, SX + 6, 4 * TY, NZ), jnp.bfloat16),
            vmem((4, SX + 6, NY, NZ), F32),
            vmem((2, SX + 5, NY, NZ), F32),
            vmem((2, SX + 4, NY, NZ), F32),
            vmem((2, SX + 4, NY, NZ), F32),
            vmem((group, SX + 8, NY, NZ), F32),
            vmem((group, SX + 4, NY, NZ), F32),
            vmem((group, SX, NY, NZ), F32),
            vmem((group, SX + 4, NY, NZ), F32),
            vmem((SX, NY, NZ), F32),
            vmem((n_tracer, SX * 8, NZ), F32),
            vmem((n_tracer, SX * 8, NZ), F32),
            vmem((2, n_tracer, 8, NZ), F32),
            vmem((19 * rows, NZ), F32),
            vmem((3 * rows, NZ), F32),
            dma((3,)),
            dma((3,)),
            dma((3, 8)),
            dma((3, 8)),
            dma((2, CHUNKS)),
            dma((2, CHUNKS)),
            dma((3, n_tracer)),
            dma((3, n_tracer)),
            dma((3, n_tracer)),
            dma((3, n_tracer)),
        ],
        compiler_params=pltpu.CompilerParams(
            collective_id=0, has_side_effects=True, vmem_limit_bytes=40 * 1024 * 1024
        ),
        name="plume",
    )(
        decay_rates,
        buoyancy_coeffs,
        source_cells.T,
        source_rates.T,
        populations.reshape(19 * rows, NZ),
        solid_mask.reshape(rows, NZ),
        tracers,
    )
    return (
        out[0].reshape(populations.shape),
        out[1].reshape((3,) + populations.shape[1:]),
        out[2],
    )


def solution(mesh):
    placed = (
        P(None, "space", "tracer", None),
        P("space", "tracer", None),
        P("tracer", "space", None, None),
        P("tracer"),
        P("tracer"),
        P("tracer", None),
        P("tracer", None),
    )
    return jax.shard_map(
        functools.partial(local, mesh.shape["space"], mesh.shape["tracer"]),
        mesh=mesh,
        in_specs=placed,
        out_specs=(
            P(None, "space", "tracer", None),
            P(None, "space", "tracer", None),
            P("tracer", "space", None, None),
        ),
        check_vma=False,
    )
```

```python
import functools

import jax
import jax.numpy as jnp
from jax import lax
from jax.experimental import pallas as pl
from jax.experimental.pallas import tpu as pltpu
from jax.sharding import PartitionSpec as P

DIRS = (
    (0, 0, 0),
    (1, 0, 0),
    (-1, 0, 0),
    (0, 1, 0),
    (0, -1, 0),
    (0, 0, 1),
    (0, 0, -1),
    (1, 1, 0),
    (-1, -1, 0),
    (1, -1, 0),
    (-1, 1, 0),
    (1, 0, 1),
    (-1, 0, -1),
    (1, 0, -1),
    (-1, 0, 1),
    (0, 1, 1),
    (0, -1, -1),
    (0, 1, -1),
    (0, -1, 1),
)
WEIGHTS = (1.0 / 3.0,) + (1.0 / 18.0,) * 6 + (1.0 / 36.0,) * 12
OPP = (0, 2, 1, 4, 3, 6, 5, 8, 7, 10, 9, 12, 11, 14, 13, 16, 15, 18, 17)
RELAX = 1.25
XD = ((1, 7, 9, 11, 13), (2, 8, 10, 12, 14))
YD = ((3, 7, 10, 15, 17), (4, 8, 9, 16, 18))
CORNERS = ((7, -1, -1), (9, -1, 1), (10, 1, -1), (8, 1, 1))
CORNER_OF = {7: 0, 9: 1, 10: 2, 8: 3}
FLAG = 5
SX, NY, NZ = 8, 16, 128
TY = 4
CHUNKS = 8
FIRST, SECOND = 3, 6
F32 = jnp.float32


def kernel(
    n_space,
    n_tracer,
    decay_hbm,
    coeff_hbm,
    cells_hbm,
    rates_hbm,
    pop_hbm,
    mask_hbm,
    tracer_hbm,
    pop_out,
    vel_out,
    tracer_out,
    decay_ref,
    coeff_ref,
    cells_ref,
    rates_ref,
    fin,
    mask_in,
    fluid_v,
    both,
    post,
    xs,
    xr,
    ys,
    yr,
    cs,
    cr,
    flow_f,
    fb,
    gflow,
    face_x,
    face_y,
    face_z,
    cext,
    outer_s,
    outer_r,
    lx,
    hx,
    ly,
    hy,
    lz,
    hz,
    base,
    csec,
    cout,
    emis,
    part,
    sb,
    rb,
    rx,
    fout,
    vout,
    load_sem,
    out_sem,
    halo_send,
    halo_recv,
    bulk_send,
    bulk_recv,
    flow_send,
    flow_recv,
    buoy_send,
    buoy_recv,
):
    sp = lax.axis_index("space")
    tr = lax.axis_index("tracer")
    space = {-1: lax.rem(sp + n_space - 1, n_space), 0: sp, 1: lax.rem(sp + 1, n_space)}
    trs = [lax.rem(tr + k, n_tracer) for k in range(n_tracer)]
    group = tracer_hbm.shape[0]
    piece = group // CHUNKS

    def rcopy(src, dst, ssem, rsem, ds, t):
        return pltpu.make_async_remote_copy(
            src_ref=src,
            dst_ref=dst,
            send_sem=ssem,
            recv_sem=rsem,
            device_id=(space[ds], t),
            device_id_type=pl.DeviceIdType.MESH,
        )

    load_pop = pltpu.make_async_copy(pop_hbm, fin, load_sem.at[0])
    load_mask = pltpu.make_async_copy(mask_hbm, mask_in, load_sem.at[1])
    load_tracer = pltpu.make_async_copy(tracer_hbm, cext.at[:, 4 : 4 + SX], load_sem.at[2])
    scalars = [
        pltpu.make_async_copy(a, b, load_sem.at[3 + i])
        for i, (a, b) in enumerate(
            (
                (cells_hbm, cells_ref),
                (rates_hbm, rates_ref),
                (decay_hbm, decay_ref),
                (coeff_hbm, coeff_ref),
            )
        )
    ]

    along_x = {-1: sp > 0, 1: sp < n_space - 1}
    along_y = {-1: tr > 0, 1: tr < n_tracer - 1}

    def where_there(ds, dt, body):
        if ds != 0 and dt != 0:
            pl.when(jnp.logical_and(along_x[ds], along_y[dt]))(body)
        elif ds != 0:
            pl.when(along_x[ds])(body)
        elif dt != 0:
            pl.when(along_y[dt])(body)
        else:
            body()

    barrier = pltpu.get_barrier_semaphore()

    def greet(ds):
        def body():
            for k in range(n_tracer):
                if (ds, k) != (0, 0):
                    pl.semaphore_signal(
                        barrier,
                        inc=1,
                        device_id=(space[ds], trs[k]),
                        device_id_type=pl.DeviceIdType.MESH,
                    )

        where_there(ds, 0, body)

    for ds in (-1, 1, 0):
        greet(ds)
    load_pop.start()
    load_mask.start()
    load_tracer.start()
    for c in scalars:
        c.start()

    def clear_x(ds):
        side = 0 if ds < 0 else 1

        @pl.when(jnp.logical_not(along_x[ds]))
        def _():
            xr[0, side, FLAG] = jnp.zeros((8, NZ), F32)
            for step in range(3):
                for k in range(5):
                    xr[step, side, k] = jnp.zeros((8, NZ), F32)
                for c in range(4):
                    if CORNERS[c][1] == ds:
                        for m in range(2):
                            cr[step, c, m] = jnp.zeros((8, NZ), F32)
            for t in range(n_tracer):
                for x in range(3):
                    fb[t, x if ds < 0 else SX + 3 + x] = jnp.zeros((4 * TY, NZ), jnp.bfloat16)
                rx[side, t] = jnp.zeros((8, NZ), F32)

            def body(t, carry):
                for x in range(2):
                    cext[t, (2 if ds < 0 else SX + 4) + x] = jnp.zeros((NY, NZ), F32)
                    outer_r[side, t, x] = jnp.zeros((NY, NZ), jnp.bfloat16)
                return carry

            lax.fori_loop(0, group, body, 0)

    def clear_y(dt):
        side = 0 if dt < 0 else 1

        @pl.when(jnp.logical_not(along_y[dt]))
        def _():
            yr[0, side, FLAG] = jnp.zeros((8, NZ), F32)
            for step in range(3):
                for k in range(5):
                    yr[step, side, k] = jnp.zeros((8, NZ), F32)
                for c in range(4):
                    if CORNERS[c][2] == dt:
                        for m in range(2):
                            cr[step, c, m] = jnp.zeros((8, NZ), F32)

    for d in (-1, 1):
        clear_x(d)
        clear_y(d)

    xi = lax.broadcasted_iota(jnp.int32, (SX, NZ), 0)
    zi = lax.broadcasted_iota(jnp.int32, (SX, NZ), 1)

    def moments(f):
        even = {}
        rho = f[0]
        u = [None, None, None]
        for q in range(1, 19, 2):
            rho = rho + (f[q] + f[q + 1])
            diff = f[q] - f[q + 1]
            for a in range(3):
                e = DIRS[q][a]
                if e == 1:
                    u[a] = diff if u[a] is None else u[a] + diff
                elif e == -1:
                    u[a] = -diff if u[a] is None else u[a] - diff
        inv = 1.0 / rho
        return rho, [v * inv for v in u]

    def collide(f, rho, u):
        base = 1.0 - 1.5 * (u[0] * u[0] + u[1] * u[1] + u[2] * u[2])
        scaled = RELAX * rho
        out = [None] * 19
        out[0] = (1.0 - RELAX) * f[0] + (WEIGHTS[0] * scaled) * base
        for q in range(1, 19, 2):
            along = None
            for a in range(3):
                e = DIRS[q][a]
                if e == 1:
                    along = u[a] if along is None else along + u[a]
                elif e == -1:
                    along = -u[a] if along is None else along - u[a]
            wr = WEIGHTS[q] * scaled
            sym = wr * (base + 4.5 * along * along)
            asym = wr * (3.0 * along)
            out[q] = (1.0 - RELAX) * f[q] + (sym + asym)
            out[q + 1] = (1.0 - RELAX) * f[q + 1] + (sym - asym)
        return out

    def keep_post(step, y, p):
        buf = step % 2
        for q in range(19):
            post[buf, q, y] = p[q]
        for k in range(5):
            xs[step, 0, k, y : y + 1, :] = p[XD[1][k]][0:1, :]
            xs[step, 1, k, y : y + 1, :] = p[XD[0][k]][SX - 1 : SX, :]
            if y == 0:
                ys[step, 0, k] = p[YD[1][k]]
            if y == TY - 1:
                ys[step, 1, k] = p[YD[0][k]]
        for c, (q, dx, dy) in enumerate(CORNERS):
            if y == (TY - 1 if dy < 0 else 0):
                row = p[q][SX - 1 : SX, :] if dx < 0 else p[q][0:1, :]
                cs[step, c, 0] = jnp.broadcast_to(row, (SX, NZ))

    def messages(step):
        part_of = pl.ds(0, 6 if step == 0 else 5)
        m = pl.ds(0, 2 if step == 0 else 1)
        out = [
            (xs.at[step, 1, part_of], xr.at[step, 0, part_of], 1, 0),
            (xs.at[step, 0, part_of], xr.at[step, 1, part_of], -1, 0),
        ]
        for c, (q, dx, dy) in enumerate(CORNERS):
            out.append((cs.at[step, c, m], cr.at[step, c, m], -dx, -dy))
        out.append((ys.at[step, 1, part_of], yr.at[step, 0, part_of], 0, 1))
        out.append((ys.at[step, 0, part_of], yr.at[step, 1, part_of], 0, -1))
        return [
            (
                rcopy(
                    s,
                    d,
                    halo_send.at[step, i],
                    halo_recv.at[step, i],
                    ds,
                    trs[dt % n_tracer],
                ),
                ds,
                dt,
            )
            for i, (s, d, ds, dt) in enumerate(out)
        ]

    def start(copies):
        for c, ds, dt in copies:
            where_there(ds, dt, c.start)

    def arrive(copies):
        for c, ds, dt in copies:
            where_there(-ds, -dt, c.wait_recv)

    def leave(copies):
        for c, ds, dt in copies:
            where_there(ds, dt, c.wait_send)

    def bulk(j):
        rows = pl.ds(j * piece, piece)
        out = []
        for i, (ds, near, there, far) in enumerate(((1, SX - 2, 2, 0), (-1, 0, SX + 4, 1))):
            out.append(
                (
                    rcopy(
                        tracer_hbm.at[rows, pl.ds(near, 2)],
                        cext.at[rows, pl.ds(there, 2)],
                        bulk_send.at[i, j],
                        bulk_recv.at[i, j],
                        ds,
                        tr,
                    ),
                    ds,
                    0,
                )
            )
            out.append(
                (
                    rcopy(
                        outer_s.at[far, rows],
                        outer_r.at[far, rows],
                        bulk_send.at[2 + i, j],
                        bulk_recv.at[2 + i, j],
                        ds,
                        tr,
                    ),
                    ds,
                    0,
                )
            )
        return out

    def start_bulk(lo, hi):
        for ds in (1, -1):

            def body():
                for j in range(lo, hi):
                    for c, d, _ in bulks[j]:
                        if d == ds:
                            c.start()

            where_there(ds, 0, body)

    def shifted(step, buf, q, y):
        ex, ey, ez = DIRS[q]
        yy = y - ey
        if yy < 0:
            v = yr[step, 0, YD[0].index(q)]
        elif yy >= TY:
            v = yr[step, 1, YD[1].index(q)]
        else:
            v = post[buf, q, yy]
        if ex != 0:
            side = 0 if ex == 1 else 1
            if 0 <= yy < TY:
                row = xr[step, side, XD[side].index(q), yy : yy + 1, :]
            else:
                row = cr[step, CORNER_OF[q], 0, 0:1, :]
            v = pltpu.roll(v, 1 if ex == 1 else SX - 1, 0)
            v = jnp.where(xi == (0 if ex == 1 else SX - 1), row, v)
        if ez != 0:
            v = pltpu.roll(v, 1 if ez == 1 else NZ - 1, 1)
        return v

    def stream(step, y):
        buf = step % 2
        air = fluid_v[y] > 0.5
        here = [post[buf, q, y] for q in range(19)]
        fresh = [here[0]]
        for q in range(1, 19):
            back = jnp.where(air, here[OPP[q]], here[q])
            fresh.append(jnp.where(both[q, y] > 0.5, shifted(step, buf, q, y), back))
        return fresh

    load_mask.wait()
    for y in range(TY):
        m = mask_in[pl.ds(y, SX, stride=TY), :]
        air = 1.0 - m.astype(F32)
        fluid_v[y] = air
        for side, x in ((0, 0), (1, SX - 1)):
            xs[0, side, FLAG, y : y + 1, :] = air[x : x + 1, :]
        if y == 0:
            ys[0, 0, FLAG] = air
        if y == TY - 1:
            ys[0, 1, FLAG] = air
        for c, (q, dx, dy) in enumerate(CORNERS):
            if y == (TY - 1 if dy < 0 else 0):
                row = air[SX - 1 : SX, :] if dx < 0 else air[0:1, :]
                cs[0, c, 1] = jnp.broadcast_to(row, (SX, NZ))
    load_pop.wait()
    for y in range(TY):
        f = [fin[pl.ds(q * SX * TY + y, SX, stride=TY), :] for q in range(19)]
        rho, u = moments(f)
        keep_post(0, y, collide(f, rho, u))

    pl.semaphore_wait(
        barrier,
        n_tracer - 1
        + n_tracer * (along_x[-1].astype(jnp.int32) + along_x[1].astype(jnp.int32)),
    )
    first = messages(0)
    start(first)

    load_tracer.wait()

    def round_outer(t, carry):
        for x in range(2):
            outer_s[1, t, x] = cext[t, 4 + 2 + x].astype(jnp.bfloat16)
            outer_s[0, t, x] = cext[t, 4 + SX - 4 + x].astype(jnp.bfloat16)
        return carry

    lax.fori_loop(0, group, round_outer, 0)
    bulks = [bulk(j) for j in range(CHUNKS)]
    start_bulk(0, FIRST)
    for c in scalars:
        c.wait()

    yi16 = lax.broadcasted_iota(jnp.int32, (NY, NZ), 0)
    zi16 = lax.broadcasted_iota(jnp.int32, (NY, NZ), 1)
    flat = yi16 * NZ + zi16
    origin = (sp * SX - 2) * (NY * NZ)

    def emit(t, carry):
        for r in range(SX + 4):
            total = jnp.zeros((NY, NZ), F32)
            for s in range(cells_ref.shape[0]):
                key = cells_ref[s, t] - (origin + r * NY * NZ)
                total = total + jnp.where(flat == key, rates_ref[s, t], 0.0)
            emis[t, r] = total
        return carry

    lax.fori_loop(0, group, emit, 0)

    arrive(first)

    for y in range(TY):
        mine = fluid_v[y]
        for q in range(1, 19):
            ex, ey, ez = DIRS[q]
            yy = y - ey
            if yy < 0:
                v = yr[0, 0, FLAG]
            elif yy >= TY:
                v = yr[0, 1, FLAG]
            else:
                v = fluid_v[yy]
            if ex != 0:
                side = 0 if ex == 1 else 1
                if 0 <= yy < TY:
                    row = xr[0, side, FLAG, yy : yy + 1, :]
                else:
                    row = cr[0, CORNER_OF[q], 1, 0:1, :]
                v = pltpu.roll(v, 1 if ex == 1 else SX - 1, 0)
                v = jnp.where(xi == (0 if ex == 1 else SX - 1), row, v)
            if ez != 0:
                v = pltpu.roll(v, 1 if ez == 1 else NZ - 1, 1)
                v = jnp.where(zi == (0 if ez == 1 else NZ - 1), 0.0, v)
            both[q, y] = v * mine

    for y in range(TY):
        f = stream(0, y)
        rho, u = moments(f)
        keep_post(1, y, collide(f, rho, u))
    second = messages(1)
    start(second)
    start_bulk(FIRST, SECOND)

    def limited(below, above):
        return 0.5 * jnp.minimum(
            jnp.maximum(below, jnp.minimum(above, 0.0)), jnp.maximum(above, 0.0)
        )

    def states(c, axis, size, index):
        above = jnp.where(index == size - 1, 0.0, pltpu.roll(c, size - 1, axis)) - c
        below = c - jnp.where(index == 0, 0.0, pltpu.roll(c, 1, axis))
        h = limited(below, above)
        return c + h, pltpu.roll(c - h, size - 1, axis)

    def reaction(t):
        before = jnp.maximum(t - 1, 0)
        return before, jnp.where(lax.rem(t, 2) == 1, decay_ref[before], 0.0), decay_ref[t]

    def prepare(j, carry):
        arrive(bulk(j))

        def one(i, carry):
            t = j * piece + i
            before, gain, rate = reaction(t)

            def row(x):
                if x < 2:
                    return outer_r[0, t, x].astype(F32)
                if x >= SX + 6:
                    return outer_r[1, t, x - SX - 6].astype(F32)
                return cext[t, x]

            c = row(1)
            below = c - row(0)
            for x in range(1, SX + 7):
                above_c = row(x + 1)
                above = above_c - c
                h = limited(below, above)
                lx[t, x - 1] = c + h
                hx[t, x - 1] = c - h
                if 2 <= x < SX + 6:
                    r = x - 2
                    ly[t, r], hy[t, r] = states(c, 0, NY, yi16)
                    lz[t, r], hz[t, r] = states(c, 1, NZ, zi16)
                    base[t, r] = c + (gain * cext[before, x] - rate * c + emis[t, r])
                c, below = above_c, above
            return carry

        return lax.fori_loop(0, piece, one, carry)

    lax.fori_loop(0, FIRST, prepare, 0)
    arrive(second)

    for y in range(TY):
        f = stream(1, y)
        rho, u = moments(f)
        air = fluid_v[y]
        for a in range(3):
            flow_f[pl.ds(a * TY + y, SX, stride=4 * TY), :] = u[a] * air
        flow_f[pl.ds(3 * TY + y, SX, stride=4 * TY), :] = air
        keep_post(2, y, collide(f, rho, u))
    for x in range(SX):
        fb[tr, 3 + x] = flow_f[x * 4 * TY : (x + 1) * 4 * TY, :].astype(jnp.bfloat16)

    kinds = {
        0: (0, pl.ds(3, SX), pl.ds(3, SX)),
        1: (1, pl.ds(SX, 3), pl.ds(0, 3)),
        -1: (2, pl.ds(3, 3), pl.ds(SX + 3, 3)),
    }

    def flow_messages(ds):
        kind, src, dst = kinds[ds]
        return [
            rcopy(
                fb.at[tr, src],
                fb.at[tr, dst],
                flow_send.at[kind, k],
                flow_recv.at[kind, tr],
                ds,
                trs[k],
            )
            for k in range(n_tracer)
            if (ds, k) != (0, 0)
        ]

    def flow_arrivals(ds):
        kind, _, rows = kinds[ds]
        return [
            rcopy(
                fb.at[trs[k], rows],
                fb.at[trs[k], rows],
                flow_send.at[kind, k],
                flow_recv.at[kind, trs[k]],
                1,
                trs[k],
            )
            for k in range(n_tracer)
            if (ds, k) != (0, 0)
        ]

    def each(copies, what):
        def body():
            for c in copies:
                getattr(c, what)()

        return body

    flows = {ds: flow_messages(ds) for ds in (1, -1, 0)}
    for ds in (1, -1, 0):
        where_there(ds, 0, each(flows[ds], "start"))
    third = messages(2)
    start(third)
    start_bulk(SECOND, CHUNKS)
    lax.fori_loop(FIRST, CHUNKS, prepare, 0)
    where_there(0, 0, each(flow_arrivals(0), "wait_recv"))

    def widen(x, carry):
        for t in range(n_tracer):
            v = fb[t, x].astype(F32)
            for a in range(4):
                gflow[a, x, t * TY : (t + 1) * TY, :] = v[a * TY : (a + 1) * TY, :]
        return carry

    def split(ref, i, s):
        ref[0, i] = jnp.maximum(s, 0.0)
        ref[1, i] = jnp.minimum(s, 0.0)

    def faces_x(i, carry):
        split(
            face_x,
            i,
            0.5 * (gflow[0, i] + gflow[0, i + 1]) * gflow[3, i] * gflow[3, i + 1],
        )
        return carry

    def faces_yz(i, carry):
        air = gflow[3, i + 1]
        v = gflow[1, i + 1]
        s = 0.5 * (v + pltpu.roll(v, NY - 1, 0)) * air * pltpu.roll(air, NY - 1, 0)
        split(face_y, i, jnp.where(yi16 == NY - 1, 0.0, s))
        v = gflow[2, i + 1]
        s = 0.5 * (v + pltpu.roll(v, NZ - 1, 1)) * air * pltpu.roll(air, NZ - 1, 1)
        split(face_z, i, jnp.where(zi16 == NZ - 1, 0.0, s))
        return carry

    lax.fori_loop(3, SX + 3, widen, 0)
    lax.fori_loop(3, SX + 2, faces_x, 0)
    lax.fori_loop(2, SX + 2, faces_yz, 0)
    for ds in (1, -1):
        where_there(-ds, 0, each(flow_arrivals(ds), "wait_recv"))
    lax.fori_loop(0, 3, widen, 0)
    lax.fori_loop(SX + 3, SX + 6, widen, 0)
    lax.fori_loop(0, 3, faces_x, 0)
    lax.fori_loop(SX + 2, SX + 5, faces_x, 0)
    lax.fori_loop(0, 2, faces_yz, 0)
    lax.fori_loop(SX + 2, SX + 4, faces_yz, 0)

    def flux_change(faces, i, left, right, axis):
        flux = faces[0, i] * left + faces[1, i] * right
        return flux - pltpu.roll(flux, 1, axis)

    def section_one(t, carry):
        low = None
        for f in range(SX + 5):
            flux = face_x[0, f] * lx[t, f] + face_x[1, f] * hx[t, f + 1]
            if f > 0:
                r = f - 1
                div = flux - low
                div = div + flux_change(face_y, r, ly[t, r], hy[t, r], 0)
                div = div + flux_change(face_z, r, lz[t, r], hz[t, r], 1)
                csec[t, r] = base[t, r] - div
            low = flux
        return carry

    lax.fori_loop(0, group, section_one, 0)

    for x in range(SX):
        part[x] = jnp.zeros((NY, NZ), F32)

    def section_two(t, lo, hi):
        before, gain, rate = reaction(t)
        weight = coeff_ref[t]
        c = csec[t, lo + 1]
        below = c - csec[t, lo]
        left = low = None
        for x in range(lo - 1, hi + 1):
            above_c = csec[t, x + 3]
            above = above_c - c
            h = limited(below, above)
            if left is not None:
                flux = face_x[0, x + 2] * left + face_x[1, x + 2] * (c - h)
                if low is not None:
                    r = x - 1
                    mid = csec[t, r + 2]
                    div = flux - low
                    i = r + 2
                    div = div + flux_change(face_y, i, *states(mid, 0, NY, yi16), 0)
                    div = div + flux_change(face_z, i, *states(mid, 1, NZ, zi16), 1)
                    made = gain * csec[before, i] - rate * mid
                    v = mid + (made - div + emis[t, i])
                    cout[t, r] = v
                    part[r] = part[r] + weight * v
                low = flux
            left = c + h
            c, below = above_c, above

    def boundary_rows(t, carry):
        section_two(t, 0, 1)
        section_two(t, SX - 1, SX)
        return carry

    def inner_rows(t, carry):
        section_two(t, 1, SX - 1)
        return carry

    def pack(x):
        v = part[x]
        for t in range(n_tracer):
            sb[t, x * 8 : (x + 1) * 8, :] = pltpu.roll(v, (1 - TY * t) % NY, 0)[0:8]

    lax.fori_loop(0, group, boundary_rows, 0)
    pack(0)
    pack(SX - 1)
    sides = {}
    for ds, rows, dst in ((1, pl.ds((SX - 1) * 8, 8), 0), (-1, pl.ds(0, 8), 1)):
        sides[ds] = [
            rcopy(
                sb.at[trs[k], rows],
                rx.at[dst, k],
                buoy_send.at[dst + 1, k],
                buoy_recv.at[dst + 1, k],
                ds,
                trs[k],
            )
            for k in range(n_tracer)
        ]
        where_there(ds, 0, each(sides[ds], "start"))
    lax.fori_loop(0, group, inner_rows, 0)
    for x in range(1, SX - 1):
        pack(x)
    buoy = [
        rcopy(sb.at[trs[k]], rb.at[k], buoy_send.at[0, k], buoy_recv.at[0, k], 0, trs[k])
        for k in range(1, n_tracer)
    ]
    each(buoy, "start")()
    save_tracer = pltpu.make_async_copy(cout, tracer_out, out_sem.at[0])
    save_tracer.start()

    arrive(third)
    for ds in (1, -1):
        where_there(-ds, 0, each(sides[ds], "wait_recv"))
    each(buoy, "wait_recv")()

    buf = 0
    for yy in range(-1, TY + 1):
        g = sb[tr, pl.ds(yy + 1, SX, stride=8), :]
        for k in range(1, n_tracer):
            g = g + rb[k, pl.ds(yy + 1, SX, stride=8), :]
        if yy < 0 or yy >= TY:
            side = 0 if yy < 0 else 1
            for k, q in enumerate(YD[side]):
                if DIRS[q][2]:
                    yr[2, side, k] = yr[2, side, k] + (3.0 * WEIGHTS[q] * DIRS[q][2]) * g
        else:
            for q in range(19):
                if DIRS[q][2]:
                    post[buf, q, yy] = post[buf, q, yy] + (3.0 * WEIGHTS[q] * DIRS[q][2]) * g
    for side in range(2):
        g = rx[side, 0]
        for k in range(1, n_tracer):
            g = g + rx[side, k]
        g = pltpu.roll(g, 7, 0)
        for k, q in enumerate(XD[side]):
            if DIRS[q][2]:
                xr[2, side, k] = xr[2, side, k] + (3.0 * WEIGHTS[q] * DIRS[q][2]) * g

    for y in range(TY):
        f = stream(2, y)
        rho, u = moments(f)
        for q in range(19):
            fout[pl.ds(q * SX * TY + y, SX, stride=TY), :] = f[q]
        for a in range(3):
            vout[pl.ds(a * SX * TY + y, SX, stride=TY), :] = u[a] * fluid_v[y]
    save_pop = pltpu.make_async_copy(fout, pop_out, out_sem.at[1])
    save_vel = pltpu.make_async_copy(vout, vel_out, out_sem.at[2])
    save_pop.start()
    save_vel.start()

    leave(first + second + third)
    for j in range(CHUNKS):
        leave(bulks[j])
    for ds in (1, -1, 0):
        where_there(ds, 0, each(flows[ds], "wait_send"))
    for ds in (1, -1):
        where_there(ds, 0, each(sides[ds], "wait_send"))
    each(buoy, "wait_send")()
    save_tracer.wait()
    save_pop.wait()
    save_vel.wait()


def local(
    n_space,
    n_tracer,
    populations,
    solid_mask,
    tracers,
    decay_rates,
    buoyancy_coeffs,
    source_cells,
    source_rates,
):
    group = tracers.shape[0]
    rows = SX * TY
    smem = pltpu.SMEM
    hbm = pl.BlockSpec(memory_space=pl.ANY)
    vmem = pltpu.VMEM
    dma = pltpu.SemaphoreType.DMA
    out = pl.pallas_call(
        functools.partial(kernel, n_space, n_tracer),
        out_shape=(
            jax.ShapeDtypeStruct((19 * rows, NZ), F32),
            jax.ShapeDtypeStruct((3 * rows, NZ), F32),
            jax.ShapeDtypeStruct(tracers.shape, F32),
        ),
        in_specs=[hbm] * 7,
        out_specs=(hbm, hbm, hbm),
        scratch_shapes=[
            smem((group,), F32),
            smem((group,), F32),
            smem(source_cells.shape[::-1], jnp.int32),
            smem(source_rates.shape[::-1], F32),
            vmem((19 * rows, NZ), F32),
            vmem((rows, NZ), jnp.int32),
            vmem((TY, SX, NZ), F32),
            vmem((19, TY, SX, NZ), F32),
            vmem((2, 19, TY, SX, NZ), F32),
            vmem((3, 2, 6, 8, NZ), F32),
            vmem((3, 2, 6, 8, NZ), F32),
            vmem((3, 2, 6, 8, NZ), F32),
            vmem((3, 2, 6, 8, NZ), F32),
            vmem((3, 4, 2, 8, NZ), F32),
            vmem((3, 4, 2, 8, NZ), F32),
            vmem((SX * 4 * TY, NZ), F32),
            vmem((n_tracer, SX + 6, 4 * TY, NZ), jnp.bfloat16),
            vmem((4, SX + 6, NY, NZ), F32),
            vmem((2, SX + 5, NY, NZ), F32),
            vmem((2, SX + 4, NY, NZ), F32),
            vmem((2, SX + 4, NY, NZ), F32),
            vmem((group, SX + 8, NY, NZ), F32),
            vmem((2, group, 2, NY, NZ), jnp.bfloat16),
            vmem((2, group, 2, NY, NZ), jnp.bfloat16),
            vmem((group, SX + 6, NY, NZ), F32),
            vmem((group, SX + 6, NY, NZ), F32),
            vmem((group, SX + 4, NY, NZ), F32),
            vmem((group, SX + 4, NY, NZ), F32),
            vmem((group, SX + 4, NY, NZ), F32),
            vmem((group, SX + 4, NY, NZ), F32),
            vmem((group, SX + 4, NY, NZ), F32),
            vmem((group, SX + 4, NY, NZ), F32),
            vmem((group, SX, NY, NZ), F32),
            vmem((group, SX + 4, NY, NZ), F32),
            vmem((SX, NY, NZ), F32),
            vmem((n_tracer, SX * 8, NZ), F32),
            vmem((n_tracer, SX * 8, NZ), F32),
            vmem((2, n_tracer, 8, NZ), F32),
            vmem((19 * rows, NZ), F32),
            vmem((3 * rows, NZ), F32),
            dma((7,)),
            dma((3,)),
            dma((3, 8)),
            dma((3, 8)),
            dma((4, CHUNKS)),
            dma((4, CHUNKS)),
            dma((3, n_tracer)),
            dma((3, n_tracer)),
            dma((3, n_tracer)),
            dma((3, n_tracer)),
        ],
        compiler_params=pltpu.CompilerParams(
            collective_id=0, has_side_effects=True, vmem_limit_bytes=67043328
        ),
        name="plume",
    )(
        decay_rates,
        buoyancy_coeffs,
        source_cells.T,
        source_rates.T,
        populations.reshape(19 * rows, NZ),
        solid_mask.reshape(rows, NZ),
        tracers,
    )
    return (
        out[0].reshape(populations.shape),
        out[1].reshape((3,) + populations.shape[1:]),
        out[2],
    )


def solution(mesh):
    placed = (
        P(None, "space", "tracer", None),
        P("space", "tracer", None),
        P("tracer", "space", None, None),
        P("tracer"),
        P("tracer"),
        P("tracer", None),
        P("tracer", None),
    )
    return jax.shard_map(
        functools.partial(local, mesh.shape["space"], mesh.shape["tracer"]),
        mesh=mesh,
        in_specs=placed,
        out_specs=(
            P(None, "space", "tracer", None),
            P(None, "space", "tracer", None),
            P("tracer", "space", None, None),
        ),
        check_vma=False,
    )
```

```python
import functools

import jax
import jax.numpy as jnp
from jax import lax
from jax.experimental import pallas as pl
from jax.experimental.pallas import tpu as pltpu
from jax.sharding import PartitionSpec as P

DIRS = (
    (0, 0, 0),
    (1, 0, 0),
    (-1, 0, 0),
    (0, 1, 0),
    (0, -1, 0),
    (0, 0, 1),
    (0, 0, -1),
    (1, 1, 0),
    (-1, -1, 0),
    (1, -1, 0),
    (-1, 1, 0),
    (1, 0, 1),
    (-1, 0, -1),
    (1, 0, -1),
    (-1, 0, 1),
    (0, 1, 1),
    (0, -1, -1),
    (0, 1, -1),
    (0, -1, 1),
)
WEIGHTS = (1.0 / 3.0,) + (1.0 / 18.0,) * 6 + (1.0 / 36.0,) * 12
OPP = (0, 2, 1, 4, 3, 6, 5, 8, 7, 10, 9, 12, 11, 14, 13, 16, 15, 18, 17)
RELAX = 1.25
XD = ((1, 7, 9, 11, 13), (2, 8, 10, 12, 14))
YD = ((3, 7, 10, 15, 17), (4, 8, 9, 16, 18))
CORNERS = ((7, -1, -1), (9, -1, 1), (10, 1, -1), (8, 1, 1))
CORNER_OF = {7: 0, 9: 1, 10: 2, 8: 3}
FLAG = 5
SX, NY, NZ = 8, 16, 128
TY = 4
CHUNKS = 8
FIRST = 4
INNER = 5
F32 = jnp.float32


def kernel(
    n_space,
    n_tracer,
    decay_hbm,
    coeff_hbm,
    cells_hbm,
    rates_hbm,
    pop_hbm,
    mask_hbm,
    tracer_hbm,
    fout,
    vout,
    cout,
    decay_ref,
    coeff_ref,
    cells_ref,
    rates_ref,
    fin,
    mask_in,
    fluid_v,
    both,
    post,
    xs,
    xr,
    ys,
    yr,
    cs,
    cr,
    flow_f,
    fb,
    gflow,
    face_x,
    face_y,
    face_z,
    cext,
    outer_s,
    outer_r,
    lx,
    hx,
    ly,
    hy,
    lz,
    hz,
    base,
    csec,
    emis,
    part,
    sb,
    rb,
    rx,
    load_sem,
    halo_send,
    halo_recv,
    bulk_send,
    bulk_recv,
    flow_send,
    flow_recv,
    buoy_send,
    buoy_recv,
):
    sp = lax.axis_index("space")
    tr = lax.axis_index("tracer")
    space = {-1: lax.rem(sp + n_space - 1, n_space), 0: sp, 1: lax.rem(sp + 1, n_space)}
    trs = [lax.rem(tr + k, n_tracer) for k in range(n_tracer)]
    group = tracer_hbm.shape[0]
    piece = group // CHUNKS

    def rcopy(src, dst, ssem, rsem, ds, t):
        return pltpu.make_async_remote_copy(
            src_ref=src,
            dst_ref=dst,
            send_sem=ssem,
            recv_sem=rsem,
            device_id=(space[ds], t),
            device_id_type=pl.DeviceIdType.MESH,
        )

    load_pop = pltpu.make_async_copy(pop_hbm, fin, load_sem.at[0])
    load_mask = pltpu.make_async_copy(mask_hbm, mask_in, load_sem.at[1])
    load_tracer = pltpu.make_async_copy(tracer_hbm, cext.at[:, 4 : 4 + SX], load_sem.at[2])
    scalars = [
        pltpu.make_async_copy(a, b, load_sem.at[3 + i])
        for i, (a, b) in enumerate(
            (
                (cells_hbm, cells_ref),
                (rates_hbm, rates_ref),
                (decay_hbm, decay_ref),
                (coeff_hbm, coeff_ref),
            )
        )
    ]

    along_x = {-1: sp > 0, 1: sp < n_space - 1}
    along_y = {-1: tr > 0, 1: tr < n_tracer - 1}

    def where_there(ds, dt, body):
        if ds != 0 and dt != 0:
            pl.when(jnp.logical_and(along_x[ds], along_y[dt]))(body)
        elif ds != 0:
            pl.when(along_x[ds])(body)
        elif dt != 0:
            pl.when(along_y[dt])(body)
        else:
            body()

    barrier = pltpu.get_barrier_semaphore()

    def greet(ds):
        def body():
            for k in range(n_tracer):
                if (ds, k) != (0, 0):
                    pl.semaphore_signal(
                        barrier,
                        inc=1,
                        device_id=(space[ds], trs[k]),
                        device_id_type=pl.DeviceIdType.MESH,
                    )

        where_there(ds, 0, body)

    for ds in (-1, 1, 0):
        greet(ds)
    load_pop.start()
    load_mask.start()
    load_tracer.start()
    for c in scalars:
        c.start()

    def clear_x(ds):
        side = 0 if ds < 0 else 1

        @pl.when(jnp.logical_not(along_x[ds]))
        def _():
            xr[0, side, FLAG] = jnp.zeros((8, NZ), F32)
            for step in range(3):
                for k in range(5):
                    xr[step, side, k] = jnp.zeros((8, NZ), F32)
                for c in range(4):
                    if CORNERS[c][1] == ds:
                        for m in range(2):
                            cr[step, c, m] = jnp.zeros((8, NZ), F32)
            for t in range(n_tracer):
                for x in range(3):
                    fb[t, x if ds < 0 else SX + 3 + x] = jnp.zeros((4 * TY, NZ), jnp.bfloat16)
                rx[side, t] = jnp.zeros((8, NZ), F32)

            def body(t, carry):
                for x in range(2):
                    cext[t, (2 if ds < 0 else SX + 4) + x] = jnp.zeros((NY, NZ), F32)
                    outer_r[side, t, x] = jnp.zeros((NY, NZ), jnp.bfloat16)
                return carry

            lax.fori_loop(0, group, body, 0)

    def clear_y(dt):
        side = 0 if dt < 0 else 1

        @pl.when(jnp.logical_not(along_y[dt]))
        def _():
            yr[0, side, FLAG] = jnp.zeros((8, NZ), F32)
            for step in range(3):
                for k in range(5):
                    yr[step, side, k] = jnp.zeros((8, NZ), F32)
                for c in range(4):
                    if CORNERS[c][2] == dt:
                        for m in range(2):
                            cr[step, c, m] = jnp.zeros((8, NZ), F32)

    for d in (-1, 1):
        clear_x(d)
        clear_y(d)

    xi = lax.broadcasted_iota(jnp.int32, (SX, NZ), 0)
    zi = lax.broadcasted_iota(jnp.int32, (SX, NZ), 1)

    def moments(f):
        even = {}
        rho = f[0]
        u = [None, None, None]
        for q in range(1, 19, 2):
            rho = rho + (f[q] + f[q + 1])
            diff = f[q] - f[q + 1]
            for a in range(3):
                e = DIRS[q][a]
                if e == 1:
                    u[a] = diff if u[a] is None else u[a] + diff
                elif e == -1:
                    u[a] = -diff if u[a] is None else u[a] - diff
        inv = 1.0 / rho
        return rho, [v * inv for v in u]

    def collide(f, rho, u):
        base = 1.0 - 1.5 * (u[0] * u[0] + u[1] * u[1] + u[2] * u[2])
        scaled = RELAX * rho
        out = [None] * 19
        out[0] = (1.0 - RELAX) * f[0] + (WEIGHTS[0] * scaled) * base
        for q in range(1, 19, 2):
            along = None
            for a in range(3):
                e = DIRS[q][a]
                if e == 1:
                    along = u[a] if along is None else along + u[a]
                elif e == -1:
                    along = -u[a] if along is None else along - u[a]
            wr = WEIGHTS[q] * scaled
            sym = wr * (base + 4.5 * along * along)
            asym = wr * (3.0 * along)
            out[q] = (1.0 - RELAX) * f[q] + (sym + asym)
            out[q + 1] = (1.0 - RELAX) * f[q + 1] + (sym - asym)
        return out

    def keep_post(step, y, p):
        buf = step % 2
        for q in range(19):
            post[buf, q, y] = p[q]
        for k in range(5):
            xs[step, 0, k, y : y + 1, :] = p[XD[1][k]][0:1, :]
            xs[step, 1, k, y : y + 1, :] = p[XD[0][k]][SX - 1 : SX, :]
            if y == 0:
                ys[step, 0, k] = p[YD[1][k]]
            if y == TY - 1:
                ys[step, 1, k] = p[YD[0][k]]
        for c, (q, dx, dy) in enumerate(CORNERS):
            if y == (TY - 1 if dy < 0 else 0):
                row = p[q][SX - 1 : SX, :] if dx < 0 else p[q][0:1, :]
                cs[step, c, 0] = jnp.broadcast_to(row, (SX, NZ))

    def messages(step):
        part_of = pl.ds(0, 6 if step == 0 else 5)
        m = pl.ds(0, 2 if step == 0 else 1)
        out = [
            (xs.at[step, 1, part_of], xr.at[step, 0, part_of], 1, 0),
            (xs.at[step, 0, part_of], xr.at[step, 1, part_of], -1, 0),
        ]
        for c, (q, dx, dy) in enumerate(CORNERS):
            out.append((cs.at[step, c, m], cr.at[step, c, m], -dx, -dy))
        out.append((ys.at[step, 1, part_of], yr.at[step, 0, part_of], 0, 1))
        out.append((ys.at[step, 0, part_of], yr.at[step, 1, part_of], 0, -1))
        return [
            (
                rcopy(
                    s,
                    d,
                    halo_send.at[step, i],
                    halo_recv.at[step, i],
                    ds,
                    trs[dt % n_tracer],
                ),
                ds,
                dt,
            )
            for i, (s, d, ds, dt) in enumerate(out)
        ]

    def start(copies):
        for c, ds, dt in copies:
            where_there(ds, dt, c.start)

    def arrive(copies):
        for c, ds, dt in copies:
            where_there(-ds, -dt, c.wait_recv)

    def leave(copies):
        for c, ds, dt in copies:
            where_there(ds, dt, c.wait_send)

    def bulk(j):
        rows = pl.ds(j * piece, piece)
        out = []
        for i, (ds, near, there, far) in enumerate(((1, SX - 2, 2, 0), (-1, 0, SX + 4, 1))):
            out.append(
                (
                    rcopy(
                        tracer_hbm.at[rows, pl.ds(near, 2)],
                        cext.at[rows, pl.ds(there, 2)],
                        bulk_send.at[i, j],
                        bulk_recv.at[i, j],
                        ds,
                        tr,
                    ),
                    ds,
                    0,
                )
            )
            out.append(
                (
                    rcopy(
                        outer_s.at[far, rows],
                        outer_r.at[far, rows],
                        bulk_send.at[2 + i, j],
                        bulk_recv.at[2 + i, j],
                        ds,
                        tr,
                    ),
                    ds,
                    0,
                )
            )
        return out

    def start_bulk(lo, hi):
        for ds in (1, -1):

            def body():
                for j in range(lo, hi):
                    for c, d, _ in bulks[j]:
                        if d == ds:
                            c.start()

            where_there(ds, 0, body)

    def shifted(step, buf, q, y):
        ex, ey, ez = DIRS[q]
        yy = y - ey
        if yy < 0:
            v = yr[step, 0, YD[0].index(q)]
        elif yy >= TY:
            v = yr[step, 1, YD[1].index(q)]
        else:
            v = post[buf, q, yy]
        if ex != 0:
            side = 0 if ex == 1 else 1
            if 0 <= yy < TY:
                row = xr[step, side, XD[side].index(q), yy : yy + 1, :]
            else:
                row = cr[step, CORNER_OF[q], 0, 0:1, :]
            v = pltpu.roll(v, 1 if ex == 1 else SX - 1, 0)
            v = jnp.where(xi == (0 if ex == 1 else SX - 1), row, v)
        if ez != 0:
            v = pltpu.roll(v, 1 if ez == 1 else NZ - 1, 1)
        return v

    def stream(step, y):
        buf = step % 2
        air = fluid_v[y] > 0.5
        here = [post[buf, q, y] for q in range(19)]
        fresh = [here[0]]
        for q in range(1, 19):
            back = jnp.where(air, here[OPP[q]], here[q])
            fresh.append(jnp.where(both[q, y] > 0.5, shifted(step, buf, q, y), back))
        return fresh

    load_mask.wait()
    for y in range(TY):
        m = mask_in[pl.ds(y, SX, stride=TY), :]
        air = 1.0 - m.astype(F32)
        fluid_v[y] = air
        for side, x in ((0, 0), (1, SX - 1)):
            xs[0, side, FLAG, y : y + 1, :] = air[x : x + 1, :]
        if y == 0:
            ys[0, 0, FLAG] = air
        if y == TY - 1:
            ys[0, 1, FLAG] = air
        for c, (q, dx, dy) in enumerate(CORNERS):
            if y == (TY - 1 if dy < 0 else 0):
                row = air[SX - 1 : SX, :] if dx < 0 else air[0:1, :]
                cs[0, c, 1] = jnp.broadcast_to(row, (SX, NZ))
    load_pop.wait()
    for y in range(TY):
        f = [fin[pl.ds(q * SX * TY + y, SX, stride=TY), :] for q in range(19)]
        rho, u = moments(f)
        keep_post(0, y, collide(f, rho, u))

    pl.semaphore_wait(
        barrier,
        n_tracer - 1
        + n_tracer * (along_x[-1].astype(jnp.int32) + along_x[1].astype(jnp.int32)),
    )
    first = messages(0)
    start(first)

    load_tracer.wait()

    def round_outer(t, carry):
        for x in range(2):
            outer_s[1, t, x] = cext[t, 4 + 2 + x].astype(jnp.bfloat16)
            outer_s[0, t, x] = cext[t, 4 + SX - 4 + x].astype(jnp.bfloat16)
        return carry

    lax.fori_loop(0, group, round_outer, 0)
    bulks = [bulk(j) for j in range(CHUNKS)]
    start_bulk(0, FIRST)
    for c in scalars:
        c.wait()

    yi16 = lax.broadcasted_iota(jnp.int32, (NY, NZ), 0)
    zi16 = lax.broadcasted_iota(jnp.int32, (NY, NZ), 1)
    flat = yi16 * NZ + zi16
    origin = (sp * SX - 2) * (NY * NZ)

    def emit(t, carry):
        for r in range(SX + 4):
            total = jnp.zeros((NY, NZ), F32)
            for s in range(cells_ref.shape[0]):
                key = cells_ref[s, t] - (origin + r * NY * NZ)
                total = total + jnp.where(flat == key, rates_ref[s, t], 0.0)
            emis[t, r] = total
        return carry

    lax.fori_loop(0, group, emit, 0)

    arrive(first)

    for y in range(TY):
        mine = fluid_v[y]
        for q in range(1, 19):
            ex, ey, ez = DIRS[q]
            yy = y - ey
            if yy < 0:
                v = yr[0, 0, FLAG]
            elif yy >= TY:
                v = yr[0, 1, FLAG]
            else:
                v = fluid_v[yy]
            if ex != 0:
                side = 0 if ex == 1 else 1
                if 0 <= yy < TY:
                    row = xr[0, side, FLAG, yy : yy + 1, :]
                else:
                    row = cr[0, CORNER_OF[q], 1, 0:1, :]
                v = pltpu.roll(v, 1 if ex == 1 else SX - 1, 0)
                v = jnp.where(xi == (0 if ex == 1 else SX - 1), row, v)
            if ez != 0:
                v = pltpu.roll(v, 1 if ez == 1 else NZ - 1, 1)
                v = jnp.where(zi == (0 if ez == 1 else NZ - 1), 0.0, v)
            both[q, y] = v * mine

    for y in range(TY):
        f = stream(0, y)
        rho, u = moments(f)
        keep_post(1, y, collide(f, rho, u))
    second = messages(1)
    start(second)
    start_bulk(FIRST, CHUNKS)

    def limited(below, above):
        return jnp.minimum(jnp.maximum(below, jnp.minimum(above, 0.0)), jnp.maximum(above, 0.0))

    def states(c, half, axis, size, index):
        above = jnp.where(index == size - 1, 0.0, pltpu.roll(half, size - 1, axis)) - half
        below = half - jnp.where(index == 0, 0.0, pltpu.roll(half, 1, axis))
        h = limited(below, above)
        return c + h, pltpu.roll(c - h, size - 1, axis)

    def reaction(t):
        before = jnp.maximum(t - 1, 0)
        return before, jnp.where(lax.rem(t, 2) == 1, decay_ref[before], 0.0), decay_ref[t]

    def ready_rows(t, row, lo, hi):
        half = 0.5 * row(lo)
        below = half - 0.5 * row(lo - 1)
        for x in range(lo, hi):
            above_half = 0.5 * row(x + 1)
            above = above_half - half
            h = limited(below, above)
            c = row(x)
            lx[t, x - 1] = c + h
            hx[t, x - 1] = c - h
            half, below = above_half, above

    def ready_planes(t, rows):
        before, gain, rate = reaction(t)
        for x in rows:
            r = x - 2
            c = cext[t, x]
            half = 0.5 * c
            ly[t, r], hy[t, r] = states(c, half, 0, NY, yi16)
            lz[t, r], hz[t, r] = states(c, half, 1, NZ, zi16)
            base[t, r] = c + (gain * cext[before, x] - rate * c + emis[t, r])

    def prepare_own(t, carry):
        ready_planes(t, range(4, SX + 4))
        ready_rows(t, lambda x: cext[t, x], 5, SX + 3)
        return carry

    def prepare_halo(j, carry):
        arrive(bulk(j))

        def one(i, carry):
            t = j * piece + i

            def row(x):
                if x < 2:
                    return outer_r[0, t, x].astype(F32)
                if x >= SX + 6:
                    return outer_r[1, t, x - SX - 6].astype(F32)
                return cext[t, x]

            ready_planes(t, (2, 3, SX + 4, SX + 5))
            ready_rows(t, row, 1, 5)
            ready_rows(t, row, SX + 3, SX + 7)
            return carry

        return lax.fori_loop(0, piece, one, carry)

    lax.fori_loop(0, group, prepare_own, 0)
    arrive(second)

    for y in range(TY):
        f = stream(1, y)
        rho, u = moments(f)
        air = fluid_v[y]
        for a in range(3):
            flow_f[pl.ds(a * TY + y, SX, stride=4 * TY), :] = u[a] * air
        flow_f[pl.ds(3 * TY + y, SX, stride=4 * TY), :] = air
        keep_post(2, y, collide(f, rho, u))
    for x in range(SX):
        fb[tr, 3 + x] = flow_f[x * 4 * TY : (x + 1) * 4 * TY, :].astype(jnp.bfloat16)

    kinds = {
        0: (0, pl.ds(3, SX), pl.ds(3, SX)),
        1: (1, pl.ds(SX, 3), pl.ds(0, 3)),
        -1: (2, pl.ds(3, 3), pl.ds(SX + 3, 3)),
    }

    def flow_messages(ds):
        kind, src, dst = kinds[ds]
        return [
            rcopy(
                fb.at[tr, src],
                fb.at[tr, dst],
                flow_send.at[kind, k],
                flow_recv.at[kind, tr],
                ds,
                trs[k],
            )
            for k in range(n_tracer)
            if (ds, k) != (0, 0)
        ]

    def flow_arrivals(ds):
        kind, _, rows = kinds[ds]
        return [
            rcopy(
                fb.at[trs[k], rows],
                fb.at[trs[k], rows],
                flow_send.at[kind, k],
                flow_recv.at[kind, trs[k]],
                1,
                trs[k],
            )
            for k in range(n_tracer)
            if (ds, k) != (0, 0)
        ]

    def each(copies, what):
        def body():
            for c in copies:
                getattr(c, what)()

        return body

    flows = {ds: flow_messages(ds) for ds in (1, -1, 0)}
    for ds in (1, -1, 0):
        where_there(ds, 0, each(flows[ds], "start"))
    third = messages(2)
    start(third)
    lax.fori_loop(0, CHUNKS, prepare_halo, 0)
    where_there(0, 0, each(flow_arrivals(0), "wait_recv"))

    def widen(x, carry):
        for t in range(n_tracer):
            v = fb[t, x].astype(F32)
            for a in range(4):
                gflow[a, x, t * TY : (t + 1) * TY, :] = v[a * TY : (a + 1) * TY, :]
        return carry

    def split(ref, i, s):
        ref[0, i] = jnp.maximum(s, 0.0)
        ref[1, i] = jnp.minimum(s, 0.0)

    def faces_x(i, carry):
        split(
            face_x,
            i,
            0.5 * (gflow[0, i] + gflow[0, i + 1]) * gflow[3, i] * gflow[3, i + 1],
        )
        return carry

    def faces_yz(i, carry):
        air = gflow[3, i + 1]
        v = gflow[1, i + 1]
        s = 0.5 * (v + pltpu.roll(v, NY - 1, 0)) * air * pltpu.roll(air, NY - 1, 0)
        split(face_y, i, jnp.where(yi16 == NY - 1, 0.0, s))
        v = gflow[2, i + 1]
        s = 0.5 * (v + pltpu.roll(v, NZ - 1, 1)) * air * pltpu.roll(air, NZ - 1, 1)
        split(face_z, i, jnp.where(zi16 == NZ - 1, 0.0, s))
        return carry

    lax.fori_loop(3, SX + 3, widen, 0)
    lax.fori_loop(3, SX + 2, faces_x, 0)
    lax.fori_loop(2, SX + 2, faces_yz, 0)
    for ds in (1, -1):
        where_there(-ds, 0, each(flow_arrivals(ds), "wait_recv"))
    lax.fori_loop(0, 3, widen, 0)
    lax.fori_loop(SX + 3, SX + 6, widen, 0)
    lax.fori_loop(0, 3, faces_x, 0)
    lax.fori_loop(SX + 2, SX + 5, faces_x, 0)
    lax.fori_loop(0, 2, faces_yz, 0)
    lax.fori_loop(SX + 2, SX + 4, faces_yz, 0)

    def flux_change(faces, i, left, right, axis):
        flux = faces[0, i] * left + faces[1, i] * right
        return flux - pltpu.roll(flux, 1, axis)

    def section_one(t, carry):
        low = None
        for f in range(SX + 5):
            flux = face_x[0, f] * lx[t, f] + face_x[1, f] * hx[t, f + 1]
            if f > 0:
                r = f - 1
                div = flux - low
                div = div + flux_change(face_y, r, ly[t, r], hy[t, r], 0)
                div = div + flux_change(face_z, r, lz[t, r], hz[t, r], 1)
                csec[t, r] = base[t, r] - div
            low = flux
        return carry

    lax.fori_loop(0, group, section_one, 0)

    for x in range(SX):
        part[x] = jnp.zeros((NY, NZ), F32)

    def section_two(t, lo, hi):
        before, gain, rate = reaction(t)
        weight = coeff_ref[t]
        half = 0.5 * csec[t, lo + 1]
        below = half - 0.5 * csec[t, lo]
        left = low = None
        for x in range(lo - 1, hi + 1):
            above_half = 0.5 * csec[t, x + 3]
            above = above_half - half
            h = limited(below, above)
            c = csec[t, x + 2]
            if left is not None:
                flux = face_x[0, x + 2] * left + face_x[1, x + 2] * (c - h)
                if low is not None:
                    r = x - 1
                    i = r + 2
                    mid = csec[t, i]
                    mid_half = 0.5 * mid
                    div = flux - low
                    div = div + flux_change(face_y, i, *states(mid, mid_half, 0, NY, yi16), 0)
                    div = div + flux_change(face_z, i, *states(mid, mid_half, 1, NZ, zi16), 1)
                    made = gain * csec[before, i] - rate * mid
                    v = mid + (made - div + emis[t, i])
                    cout[t, r] = v
                    part[r] = part[r] + weight * v
                low = flux
            left = c + h
            half, below = above_half, above

    def boundary_rows(t, carry):
        section_two(t, 0, 1)
        section_two(t, SX - 1, SX)
        return carry

    def lower_rows(t, carry):
        section_two(t, 1, INNER)
        return carry

    def upper_rows(t, carry):
        section_two(t, INNER, SX - 1)
        return carry

    def pack(x):
        v = part[x]
        for t in range(n_tracer):
            sb[t, x * 8 : (x + 1) * 8, :] = pltpu.roll(v, (1 - TY * t) % NY, 0)[0:8]

    def to_owners(i, lo, hi):
        rows = pl.ds(lo * 8, (hi - lo) * 8)
        return [
            rcopy(
                sb.at[trs[k], rows],
                rb.at[k, rows],
                buoy_send.at[2 + i, k],
                buoy_recv.at[2 + i, k],
                0,
                trs[k],
            )
            for k in range(1, n_tracer)
        ]

    buoy = [
        to_owners(i, lo, hi)
        for i, (lo, hi) in enumerate(((0, 1), (SX - 1, SX), (1, INNER), (INNER, SX - 1)))
    ]
    lax.fori_loop(0, group, boundary_rows, 0)
    pack(0)
    pack(SX - 1)
    sides = {}
    for ds, rows, dst in ((1, pl.ds((SX - 1) * 8, 8), 0), (-1, pl.ds(0, 8), 1)):
        sides[ds] = [
            rcopy(
                sb.at[trs[k], rows],
                rx.at[dst, k],
                buoy_send.at[dst, k],
                buoy_recv.at[dst, k],
                ds,
                trs[k],
            )
            for k in range(n_tracer)
        ]
        where_there(ds, 0, each(sides[ds], "start"))
    each(buoy[0] + buoy[1], "start")()
    lax.fori_loop(0, group, lower_rows, 0)
    for x in range(1, INNER):
        pack(x)
    each(buoy[2], "start")()
    lax.fori_loop(0, group, upper_rows, 0)
    for x in range(INNER, SX - 1):
        pack(x)
    each(buoy[3], "start")()
    arrive(third)
    leave(first + second + third)
    for j in range(CHUNKS):
        leave(bulks[j])
    for ds in (1, -1, 0):
        where_there(ds, 0, each(flows[ds], "wait_send"))
    for ds in (1, -1):
        where_there(ds, 0, each(sides[ds], "wait_send"))
    for ds in (1, -1):
        where_there(-ds, 0, each(sides[ds], "wait_recv"))
    each([c for row in buoy for c in row], "wait_recv")()

    buf = 0
    for yy in range(-1, TY + 1):
        g = sb[tr, pl.ds(yy + 1, SX, stride=8), :]
        for k in range(1, n_tracer):
            g = g + rb[k, pl.ds(yy + 1, SX, stride=8), :]
        if yy < 0 or yy >= TY:
            side = 0 if yy < 0 else 1
            for k, q in enumerate(YD[side]):
                if DIRS[q][2]:
                    yr[2, side, k] = yr[2, side, k] + (3.0 * WEIGHTS[q] * DIRS[q][2]) * g
        else:
            for q in range(19):
                if DIRS[q][2]:
                    post[buf, q, yy] = post[buf, q, yy] + (3.0 * WEIGHTS[q] * DIRS[q][2]) * g
    for side in range(2):
        g = rx[side, 0]
        for k in range(1, n_tracer):
            g = g + rx[side, k]
        g = pltpu.roll(g, 7, 0)
        for k, q in enumerate(XD[side]):
            if DIRS[q][2]:
                xr[2, side, k] = xr[2, side, k] + (3.0 * WEIGHTS[q] * DIRS[q][2]) * g

    for y in range(TY):
        f = stream(2, y)
        rho, u = moments(f)
        for q in range(19):
            fout[pl.ds(q * SX * TY + y, SX, stride=TY), :] = f[q]
        for a in range(3):
            vout[pl.ds(a * SX * TY + y, SX, stride=TY), :] = u[a] * fluid_v[y]

    each([c for row in buoy for c in row], "wait_send")()


def hand_over(pop_in, vel_in, tracer_in, pop_out, vel_out, tracer_out, sem):
    copies = [
        pltpu.make_async_copy(a, b, sem.at[i])
        for i, (a, b) in enumerate(
            ((tracer_in, tracer_out), (pop_in, pop_out), (vel_in, vel_out))
        )
    ]
    for c in copies:
        c.start()
    for c in copies:
        c.wait()


def local(
    n_space,
    n_tracer,
    populations,
    solid_mask,
    tracers,
    decay_rates,
    buoyancy_coeffs,
    source_cells,
    source_rates,
):
    group = tracers.shape[0]
    rows = SX * TY
    smem = pltpu.SMEM
    hbm = pl.BlockSpec(memory_space=pl.ANY)
    vmem = pltpu.VMEM
    dma = pltpu.SemaphoreType.DMA
    out = pl.pallas_call(
        functools.partial(kernel, n_space, n_tracer),
        out_shape=(
            vmem((19 * rows, NZ), F32),
            vmem((3 * rows, NZ), F32),
            vmem(tracers.shape, F32),
        ),
        in_specs=[pl.BlockSpec(memory_space=pltpu.HBM)] * 7,
        out_specs=(pl.BlockSpec(memory_space=pltpu.VMEM),) * 3,
        scratch_shapes=[
            smem((group,), F32),
            smem((group,), F32),
            smem(source_cells.shape[::-1], jnp.int32),
            smem(source_rates.shape[::-1], F32),
            vmem((19 * rows, NZ), F32),
            vmem((rows, NZ), jnp.int32),
            vmem((TY, SX, NZ), F32),
            vmem((19, TY, SX, NZ), F32),
            vmem((2, 19, TY, SX, NZ), F32),
            vmem((3, 2, 6, 8, NZ), F32),
            vmem((3, 2, 6, 8, NZ), F32),
            vmem((3, 2, 6, 8, NZ), F32),
            vmem((3, 2, 6, 8, NZ), F32),
            vmem((3, 4, 2, 8, NZ), F32),
            vmem((3, 4, 2, 8, NZ), F32),
            vmem((SX * 4 * TY, NZ), F32),
            vmem((n_tracer, SX + 6, 4 * TY, NZ), jnp.bfloat16),
            vmem((4, SX + 6, NY, NZ), F32),
            vmem((2, SX + 5, NY, NZ), F32),
            vmem((2, SX + 4, NY, NZ), F32),
            vmem((2, SX + 4, NY, NZ), F32),
            vmem((group, SX + 8, NY, NZ), F32),
            vmem((2, group, 2, NY, NZ), jnp.bfloat16),
            vmem((2, group, 2, NY, NZ), jnp.bfloat16),
            vmem((group, SX + 6, NY, NZ), F32),
            vmem((group, SX + 6, NY, NZ), F32),
            vmem((group, SX + 4, NY, NZ), F32),
            vmem((group, SX + 4, NY, NZ), F32),
            vmem((group, SX + 4, NY, NZ), F32),
            vmem((group, SX + 4, NY, NZ), F32),
            vmem((group, SX + 4, NY, NZ), F32),
            vmem((group, SX + 4, NY, NZ), F32),
            vmem((group, SX + 4, NY, NZ), F32),
            vmem((SX, NY, NZ), F32),
            vmem((n_tracer, SX * 8, NZ), F32),
            vmem((n_tracer, SX * 8, NZ), F32),
            vmem((2, n_tracer, 8, NZ), F32),
            dma((7,)),
            dma((3, 8)),
            dma((3, 8)),
            dma((4, CHUNKS)),
            dma((4, CHUNKS)),
            dma((3, n_tracer)),
            dma((3, n_tracer)),
            dma((6, n_tracer)),
            dma((6, n_tracer)),
        ],
        compiler_params=pltpu.CompilerParams(
            collective_id=0, has_side_effects=True, vmem_limit_bytes=65400000
        ),
        name="plume",
    )(
        decay_rates,
        buoyancy_coeffs,
        source_cells.T,
        source_rates.T,
        populations.reshape(19 * rows, NZ),
        solid_mask.reshape(rows, NZ),
        tracers,
    )
    out = pl.pallas_call(
        hand_over,
        out_shape=tuple(jax.ShapeDtypeStruct(v.shape, v.dtype) for v in out),
        in_specs=[hbm] * 3,
        out_specs=(hbm,) * 3,
        scratch_shapes=[dma((3,))],
        compiler_params=pltpu.CompilerParams(vmem_limit_bytes=1024 * 1024),
        name="hand_over",
    )(*out)
    return (
        out[0].reshape(populations.shape),
        out[1].reshape((3,) + populations.shape[1:]),
        out[2],
    )


def solution(mesh):
    placed = (
        P(None, "space", "tracer", None),
        P("space", "tracer", None),
        P("tracer", "space", None, None),
        P("tracer"),
        P("tracer"),
        P("tracer", None),
        P("tracer", None),
    )
    return jax.shard_map(
        functools.partial(local, mesh.shape["space"], mesh.shape["tracer"]),
        mesh=mesh,
        in_specs=placed,
        out_specs=(
            P(None, "space", "tracer", None),
            P(None, "space", "tracer", None),
            P("tracer", "space", None, None),
        ),
        check_vma=False,
    )
```

```python
import functools

import jax
import jax.numpy as jnp
from jax import lax
from jax.experimental import pallas as pl
from jax.experimental.pallas import tpu as pltpu
from jax.sharding import PartitionSpec as P

DIRS = (
    (0, 0, 0),
    (1, 0, 0),
    (-1, 0, 0),
    (0, 1, 0),
    (0, -1, 0),
    (0, 0, 1),
    (0, 0, -1),
    (1, 1, 0),
    (-1, -1, 0),
    (1, -1, 0),
    (-1, 1, 0),
    (1, 0, 1),
    (-1, 0, -1),
    (1, 0, -1),
    (-1, 0, 1),
    (0, 1, 1),
    (0, -1, -1),
    (0, 1, -1),
    (0, -1, 1),
)
WEIGHTS = (1.0 / 3.0,) + (1.0 / 18.0,) * 6 + (1.0 / 36.0,) * 12
OPP = (0, 2, 1, 4, 3, 6, 5, 8, 7, 10, 9, 12, 11, 14, 13, 16, 15, 18, 17)
RELAX = 1.25
XD = ((1, 7, 9, 11, 13), (2, 8, 10, 12, 14))
YD = ((3, 7, 10, 15, 17), (4, 8, 9, 16, 18))
CORNERS = ((7, -1, -1), (9, -1, 1), (10, 1, -1), (8, 1, 1))
CORNER_OF = {7: 0, 9: 1, 10: 2, 8: 3}
FLAG = 5
SX, NY, NZ = 8, 16, 128
TY = 4
CHUNKS = 8
FIRST = 4
F32 = jnp.float32


def kernel(
    n_space,
    n_tracer,
    decay_hbm,
    coeff_hbm,
    cells_hbm,
    rates_hbm,
    pop_hbm,
    mask_hbm,
    tracer_hbm,
    fout,
    vout,
    cout,
    decay_ref,
    coeff_ref,
    cells_ref,
    rates_ref,
    fin,
    mask_in,
    fluid_v,
    both,
    post,
    xs,
    xr,
    ys,
    yr,
    cs,
    cr,
    flow_f,
    fb,
    gflow,
    face_x,
    face_y,
    face_z,
    cext,
    outer_s,
    outer_r,
    lx,
    hx,
    ly,
    hy,
    lz,
    hz,
    base,
    csec,
    emis,
    part,
    sb,
    rb,
    rx,
    load_sem,
    halo_send,
    halo_recv,
    bulk_send,
    bulk_recv,
    flow_send,
    flow_recv,
    buoy_send,
    buoy_recv,
):
    sp = lax.axis_index("space")
    tr = lax.axis_index("tracer")
    space = {-1: lax.rem(sp + n_space - 1, n_space), 0: sp, 1: lax.rem(sp + 1, n_space)}
    trs = [lax.rem(tr + k, n_tracer) for k in range(n_tracer)]
    group = tracer_hbm.shape[0]
    piece = group // CHUNKS

    def rcopy(src, dst, ssem, rsem, ds, t):
        return pltpu.make_async_remote_copy(
            src_ref=src,
            dst_ref=dst,
            send_sem=ssem,
            recv_sem=rsem,
            device_id=(space[ds], t),
            device_id_type=pl.DeviceIdType.MESH,
        )

    load_pop = pltpu.make_async_copy(pop_hbm, fin, load_sem.at[0])
    load_mask = pltpu.make_async_copy(mask_hbm, mask_in, load_sem.at[1])
    load_tracer = pltpu.make_async_copy(tracer_hbm, cext.at[:, 4 : 4 + SX], load_sem.at[2])
    scalars = [
        pltpu.make_async_copy(a, b, load_sem.at[3 + i])
        for i, (a, b) in enumerate(
            (
                (cells_hbm, cells_ref),
                (rates_hbm, rates_ref),
                (decay_hbm, decay_ref),
                (coeff_hbm, coeff_ref),
            )
        )
    ]

    along_x = {-1: sp > 0, 1: sp < n_space - 1}
    along_y = {-1: tr > 0, 1: tr < n_tracer - 1}

    def where_there(ds, dt, body):
        if ds != 0 and dt != 0:
            pl.when(jnp.logical_and(along_x[ds], along_y[dt]))(body)
        elif ds != 0:
            pl.when(along_x[ds])(body)
        elif dt != 0:
            pl.when(along_y[dt])(body)
        else:
            body()

    barrier = pltpu.get_barrier_semaphore()

    def greet(ds):
        def body():
            for k in range(n_tracer):
                if (ds, k) != (0, 0):
                    pl.semaphore_signal(
                        barrier,
                        inc=1,
                        device_id=(space[ds], trs[k]),
                        device_id_type=pl.DeviceIdType.MESH,
                    )

        where_there(ds, 0, body)

    for ds in (-1, 1, 0):
        greet(ds)
    load_pop.start()
    load_mask.start()
    load_tracer.start()
    for c in scalars:
        c.start()

    def clear_x(ds):
        side = 0 if ds < 0 else 1

        @pl.when(jnp.logical_not(along_x[ds]))
        def _():
            xr[0, side, FLAG] = jnp.zeros((8, NZ), F32)
            for step in range(3):
                for k in range(5):
                    xr[step, side, k] = jnp.zeros((8, NZ), F32)
                for c in range(4):
                    if CORNERS[c][1] == ds:
                        for m in range(2):
                            cr[step, c, m] = jnp.zeros((8, NZ), F32)
            for t in range(n_tracer):
                for x in range(3):
                    fb[t, x if ds < 0 else SX + 3 + x] = jnp.zeros((4 * TY, NZ), jnp.bfloat16)
                rx[side, t] = jnp.zeros((8, NZ), F32)

            def body(t, carry):
                for x in range(2):
                    cext[t, (2 if ds < 0 else SX + 4) + x] = jnp.zeros((NY, NZ), F32)
                    outer_r[side, t, x] = jnp.zeros((NY, NZ), jnp.bfloat16)
                return carry

            lax.fori_loop(0, group, body, 0)

    def clear_y(dt):
        side = 0 if dt < 0 else 1

        @pl.when(jnp.logical_not(along_y[dt]))
        def _():
            yr[0, side, FLAG] = jnp.zeros((8, NZ), F32)
            for step in range(3):
                for k in range(5):
                    yr[step, side, k] = jnp.zeros((8, NZ), F32)
                for c in range(4):
                    if CORNERS[c][2] == dt:
                        for m in range(2):
                            cr[step, c, m] = jnp.zeros((8, NZ), F32)

    for d in (-1, 1):
        clear_x(d)
        clear_y(d)

    xi = lax.broadcasted_iota(jnp.int32, (SX, NZ), 0)
    zi = lax.broadcasted_iota(jnp.int32, (SX, NZ), 1)

    def moments(f):
        even = {}
        rho = f[0]
        u = [None, None, None]
        for q in range(1, 19, 2):
            rho = rho + (f[q] + f[q + 1])
            diff = f[q] - f[q + 1]
            for a in range(3):
                e = DIRS[q][a]
                if e == 1:
                    u[a] = diff if u[a] is None else u[a] + diff
                elif e == -1:
                    u[a] = -diff if u[a] is None else u[a] - diff
        inv = 1.0 / rho
        return rho, [v * inv for v in u]

    def collide(f, rho, u):
        base = 1.0 - 1.5 * (u[0] * u[0] + u[1] * u[1] + u[2] * u[2])
        scaled = RELAX * rho
        out = [None] * 19
        out[0] = (1.0 - RELAX) * f[0] + (WEIGHTS[0] * scaled) * base
        for q in range(1, 19, 2):
            along = None
            for a in range(3):
                e = DIRS[q][a]
                if e == 1:
                    along = u[a] if along is None else along + u[a]
                elif e == -1:
                    along = -u[a] if along is None else along - u[a]
            wr = WEIGHTS[q] * scaled
            sym = wr * (base + 4.5 * along * along)
            asym = wr * (3.0 * along)
            out[q] = (1.0 - RELAX) * f[q] + (sym + asym)
            out[q + 1] = (1.0 - RELAX) * f[q + 1] + (sym - asym)
        return out

    def keep_post(step, y, p):
        buf = step % 2
        for q in range(19):
            post[buf, q, y] = p[q]
        for k in range(5):
            xs[step, 0, k, y : y + 1, :] = p[XD[1][k]][0:1, :]
            xs[step, 1, k, y : y + 1, :] = p[XD[0][k]][SX - 1 : SX, :]
            if y == 0:
                ys[step, 0, k] = p[YD[1][k]]
            if y == TY - 1:
                ys[step, 1, k] = p[YD[0][k]]
        for c, (q, dx, dy) in enumerate(CORNERS):
            if y == (TY - 1 if dy < 0 else 0):
                row = p[q][SX - 1 : SX, :] if dx < 0 else p[q][0:1, :]
                cs[step, c, 0] = jnp.broadcast_to(row, (SX, NZ))

    def messages(step):
        part_of = pl.ds(0, 6 if step == 0 else 5)
        m = pl.ds(0, 2 if step == 0 else 1)
        out = [
            (xs.at[step, 1, part_of], xr.at[step, 0, part_of], 1, 0),
            (xs.at[step, 0, part_of], xr.at[step, 1, part_of], -1, 0),
        ]
        for c, (q, dx, dy) in enumerate(CORNERS):
            out.append((cs.at[step, c, m], cr.at[step, c, m], -dx, -dy))
        out.append((ys.at[step, 1, part_of], yr.at[step, 0, part_of], 0, 1))
        out.append((ys.at[step, 0, part_of], yr.at[step, 1, part_of], 0, -1))
        return [
            (
                rcopy(
                    s,
                    d,
                    halo_send.at[step, i],
                    halo_recv.at[step, i],
                    ds,
                    trs[dt % n_tracer],
                ),
                ds,
                dt,
            )
            for i, (s, d, ds, dt) in enumerate(out)
        ]

    def start(copies):
        for c, ds, dt in copies:
            where_there(ds, dt, c.start)

    def arrive(copies):
        for c, ds, dt in copies:
            where_there(-ds, -dt, c.wait_recv)

    def leave(copies):
        for c, ds, dt in copies:
            where_there(ds, dt, c.wait_send)

    def bulk(j):
        rows = pl.ds(j * piece, piece)
        out = []
        for i, (ds, near, there, far) in enumerate(((1, SX - 2, 2, 0), (-1, 0, SX + 4, 1))):
            out.append(
                (
                    rcopy(
                        tracer_hbm.at[rows, pl.ds(near, 2)],
                        cext.at[rows, pl.ds(there, 2)],
                        bulk_send.at[i, j],
                        bulk_recv.at[i, j],
                        ds,
                        tr,
                    ),
                    ds,
                    0,
                )
            )
            out.append(
                (
                    rcopy(
                        outer_s.at[far, rows],
                        outer_r.at[far, rows],
                        bulk_send.at[2 + i, j],
                        bulk_recv.at[2 + i, j],
                        ds,
                        tr,
                    ),
                    ds,
                    0,
                )
            )
        return out

    def start_bulk(lo, hi):
        for ds in (1, -1):

            def body():
                for j in range(lo, hi):
                    for c, d, _ in bulks[j]:
                        if d == ds:
                            c.start()

            where_there(ds, 0, body)

    def shifted(step, buf, q, y):
        ex, ey, ez = DIRS[q]
        yy = y - ey
        if yy < 0:
            v = yr[step, 0, YD[0].index(q)]
        elif yy >= TY:
            v = yr[step, 1, YD[1].index(q)]
        else:
            v = post[buf, q, yy]
        if ex != 0:
            side = 0 if ex == 1 else 1
            if 0 <= yy < TY:
                row = xr[step, side, XD[side].index(q), yy : yy + 1, :]
            else:
                row = cr[step, CORNER_OF[q], 0, 0:1, :]
            v = pltpu.roll(v, 1 if ex == 1 else SX - 1, 0)
            v = jnp.where(xi == (0 if ex == 1 else SX - 1), row, v)
        if ez != 0:
            v = pltpu.roll(v, 1 if ez == 1 else NZ - 1, 1)
        return v

    def stream(step, y):
        buf = step % 2
        air = fluid_v[y] > 0.5
        here = [post[buf, q, y] for q in range(19)]
        fresh = [here[0]]
        for q in range(1, 19):
            back = jnp.where(air, here[OPP[q]], here[q])
            fresh.append(jnp.where(both[q, y] > 0.5, shifted(step, buf, q, y), back))
        return fresh

    load_mask.wait()
    for y in range(TY):
        m = mask_in[pl.ds(y, SX, stride=TY), :]
        air = 1.0 - m.astype(F32)
        fluid_v[y] = air
        for side, x in ((0, 0), (1, SX - 1)):
            xs[0, side, FLAG, y : y + 1, :] = air[x : x + 1, :]
        if y == 0:
            ys[0, 0, FLAG] = air
        if y == TY - 1:
            ys[0, 1, FLAG] = air
        for c, (q, dx, dy) in enumerate(CORNERS):
            if y == (TY - 1 if dy < 0 else 0):
                row = air[SX - 1 : SX, :] if dx < 0 else air[0:1, :]
                cs[0, c, 1] = jnp.broadcast_to(row, (SX, NZ))
    load_pop.wait()
    for y in range(TY):
        f = [fin[pl.ds(q * SX * TY + y, SX, stride=TY), :] for q in range(19)]
        rho, u = moments(f)
        keep_post(0, y, collide(f, rho, u))

    pl.semaphore_wait(
        barrier,
        n_tracer - 1
        + n_tracer * (along_x[-1].astype(jnp.int32) + along_x[1].astype(jnp.int32)),
    )
    first = messages(0)
    start(first)

    load_tracer.wait()

    def round_outer(t, carry):
        for x in range(2):
            outer_s[1, t, x] = cext[t, 4 + 2 + x].astype(jnp.bfloat16)
            outer_s[0, t, x] = cext[t, 4 + SX - 4 + x].astype(jnp.bfloat16)
        return carry

    lax.fori_loop(0, group, round_outer, 0)
    bulks = [bulk(j) for j in range(CHUNKS)]
    start_bulk(0, FIRST)
    for c in scalars:
        c.wait()

    yi16 = lax.broadcasted_iota(jnp.int32, (NY, NZ), 0)
    zi16 = lax.broadcasted_iota(jnp.int32, (NY, NZ), 1)
    flat = yi16 * NZ + zi16
    origin = (sp * SX - 2) * (NY * NZ)

    def emit(t, carry):
        for r in range(SX + 4):
            total = jnp.zeros((NY, NZ), F32)
            for s in range(cells_ref.shape[0]):
                key = cells_ref[s, t] - (origin + r * NY * NZ)
                total = total + jnp.where(flat == key, rates_ref[s, t], 0.0)
            emis[t, r] = total
        return carry

    lax.fori_loop(0, group, emit, 0)

    arrive(first)

    for y in range(TY):
        mine = fluid_v[y]
        for q in range(1, 19):
            ex, ey, ez = DIRS[q]
            yy = y - ey
            if yy < 0:
                v = yr[0, 0, FLAG]
            elif yy >= TY:
                v = yr[0, 1, FLAG]
            else:
                v = fluid_v[yy]
            if ex != 0:
                side = 0 if ex == 1 else 1
                if 0 <= yy < TY:
                    row = xr[0, side, FLAG, yy : yy + 1, :]
                else:
                    row = cr[0, CORNER_OF[q], 1, 0:1, :]
                v = pltpu.roll(v, 1 if ex == 1 else SX - 1, 0)
                v = jnp.where(xi == (0 if ex == 1 else SX - 1), row, v)
            if ez != 0:
                v = pltpu.roll(v, 1 if ez == 1 else NZ - 1, 1)
                v = jnp.where(zi == (0 if ez == 1 else NZ - 1), 0.0, v)
            both[q, y] = v * mine

    for y in range(TY):
        f = stream(0, y)
        rho, u = moments(f)
        keep_post(1, y, collide(f, rho, u))
    second = messages(1)
    start(second)
    start_bulk(FIRST, CHUNKS)

    def limited(below, above):
        return jnp.minimum(jnp.maximum(below, jnp.minimum(above, 0.0)), jnp.maximum(above, 0.0))

    def states(c, half, axis, size, index):
        above = jnp.where(index == size - 1, 0.0, pltpu.roll(half, size - 1, axis)) - half
        below = half - jnp.where(index == 0, 0.0, pltpu.roll(half, 1, axis))
        h = limited(below, above)
        return c + h, pltpu.roll(c - h, size - 1, axis)

    def reaction(t):
        before = jnp.maximum(t - 1, 0)
        return before, jnp.where(lax.rem(t, 2) == 1, decay_ref[before], 0.0), decay_ref[t]

    def ready_rows(t, row, lo, hi):
        half = 0.5 * row(lo)
        below = half - 0.5 * row(lo - 1)
        for x in range(lo, hi):
            above_half = 0.5 * row(x + 1)
            above = above_half - half
            h = limited(below, above)
            c = row(x)
            lx[t, x - 1] = c + h
            hx[t, x - 1] = c - h
            half, below = above_half, above

    def ready_planes(t, rows):
        before, gain, rate = reaction(t)
        for x in rows:
            r = x - 2
            c = cext[t, x]
            half = 0.5 * c
            ly[t, r], hy[t, r] = states(c, half, 0, NY, yi16)
            lz[t, r], hz[t, r] = states(c, half, 1, NZ, zi16)
            base[t, r] = c + (gain * cext[before, x] - rate * c + emis[t, r])

    def prepare_own(t, carry):
        ready_planes(t, range(4, SX + 4))
        ready_rows(t, lambda x: cext[t, x], 5, SX + 3)
        return carry

    def prepare_halo(j, carry):
        arrive(bulk(j))

        def one(i, carry):
            t = j * piece + i

            def row(x):
                if x < 2:
                    return outer_r[0, t, x].astype(F32)
                if x >= SX + 6:
                    return outer_r[1, t, x - SX - 6].astype(F32)
                return cext[t, x]

            ready_planes(t, (2, 3, SX + 4, SX + 5))
            ready_rows(t, row, 1, 5)
            ready_rows(t, row, SX + 3, SX + 7)
            return carry

        return lax.fori_loop(0, piece, one, carry)

    lax.fori_loop(0, group, prepare_own, 0)
    arrive(second)

    for y in range(TY):
        f = stream(1, y)
        rho, u = moments(f)
        air = fluid_v[y]
        for a in range(3):
            flow_f[pl.ds(a * TY + y, SX, stride=4 * TY), :] = u[a] * air
        flow_f[pl.ds(3 * TY + y, SX, stride=4 * TY), :] = air
        keep_post(2, y, collide(f, rho, u))
    for x in range(SX):
        fb[tr, 3 + x] = flow_f[x * 4 * TY : (x + 1) * 4 * TY, :].astype(jnp.bfloat16)

    kinds = {
        0: (0, pl.ds(3, SX), pl.ds(3, SX)),
        1: (1, pl.ds(SX, 3), pl.ds(0, 3)),
        -1: (2, pl.ds(3, 3), pl.ds(SX + 3, 3)),
    }

    def flow_messages(ds):
        kind, src, dst = kinds[ds]
        return [
            rcopy(
                fb.at[tr, src],
                fb.at[tr, dst],
                flow_send.at[kind, k],
                flow_recv.at[kind, tr],
                ds,
                trs[k],
            )
            for k in range(n_tracer)
            if (ds, k) != (0, 0)
        ]

    def flow_arrivals(ds):
        kind, _, rows = kinds[ds]
        return [
            rcopy(
                fb.at[trs[k], rows],
                fb.at[trs[k], rows],
                flow_send.at[kind, k],
                flow_recv.at[kind, trs[k]],
                1,
                trs[k],
            )
            for k in range(n_tracer)
            if (ds, k) != (0, 0)
        ]

    def each(copies, what):
        def body():
            for c in copies:
                getattr(c, what)()

        return body

    flows = {ds: flow_messages(ds) for ds in (1, -1, 0)}
    for ds in (1, -1, 0):
        where_there(ds, 0, each(flows[ds], "start"))
    third = messages(2)
    start(third)
    lax.fori_loop(0, CHUNKS, prepare_halo, 0)
    where_there(0, 0, each(flow_arrivals(0), "wait_recv"))

    def widen(x):
        for t in range(n_tracer):
            v = fb[t, x].astype(F32)
            for a in range(4):
                gflow[a, x, t * TY : (t + 1) * TY, :] = v[a * TY : (a + 1) * TY, :]

    def split(ref, i, s):
        ref[0, i] = jnp.maximum(s, 0.0)
        ref[1, i] = jnp.minimum(s, 0.0)

    def faces_x(i):
        split(
            face_x,
            i,
            0.5 * (gflow[0, i] + gflow[0, i + 1]) * gflow[3, i] * gflow[3, i + 1],
        )

    def faces_yz(i):
        air = gflow[3, i + 1]
        v = gflow[1, i + 1]
        s = 0.5 * (v + pltpu.roll(v, NY - 1, 0)) * air * pltpu.roll(air, NY - 1, 0)
        split(face_y, i, jnp.where(yi16 == NY - 1, 0.0, s))
        v = gflow[2, i + 1]
        s = 0.5 * (v + pltpu.roll(v, NZ - 1, 1)) * air * pltpu.roll(air, NZ - 1, 1)
        split(face_z, i, jnp.where(zi16 == NZ - 1, 0.0, s))

    for i in range(3, SX + 3):
        widen(i)
    for i in range(3, SX + 2):
        faces_x(i)
    for i in range(2, SX + 2):
        faces_yz(i)
    def flux_change(faces, i, left, right, axis):
        flux = faces[0, i] * left + faces[1, i] * right
        return flux - pltpu.roll(flux, 1, axis)

    def section_one(t, lo, hi):
        low = None
        rows = {}
        for f in range(lo, hi + 1):
            flux = face_x[0, f] * lx[t, f] + face_x[1, f] * hx[t, f + 1]
            if f > lo:
                r = f - 1
                div = flux - low
                div = div + flux_change(face_y, r, ly[t, r], hy[t, r], 0)
                div = div + flux_change(face_z, r, lz[t, r], hz[t, r], 1)
                rows[r] = base[t, r] - div
                csec[t, r] = rows[r]
            low = flux
        return rows

    for x in range(SX):
        part[x] = jnp.zeros((NY, NZ), F32)

    def section_two(t, lo, hi, rows):
        def at(r):
            return rows[r] if r in rows else csec[t, r]

        before, gain, rate = reaction(t)
        weight = coeff_ref[t]
        half = 0.5 * at(lo + 1)
        below = half - 0.5 * at(lo)
        left = low = None
        for x in range(lo - 1, hi + 1):
            above_half = 0.5 * at(x + 3)
            above = above_half - half
            h = limited(below, above)
            c = at(x + 2)
            if left is not None:
                flux = face_x[0, x + 2] * left + face_x[1, x + 2] * (c - h)
                if low is not None:
                    r = x - 1
                    i = r + 2
                    mid = at(i)
                    mid_half = 0.5 * mid
                    div = flux - low
                    div = div + flux_change(face_y, i, *states(mid, mid_half, 0, NY, yi16), 0)
                    div = div + flux_change(face_z, i, *states(mid, mid_half, 1, NZ, zi16), 1)
                    made = gain * csec[before, i] - rate * mid
                    v = mid + (made - div + emis[t, i])
                    cout[t, r] = v
                    part[r] = part[r] + weight * v
                low = flux
            left = c + h
            half, below = above_half, above

    def in_pairs(body):
        def pair(i, carry):
            body(2 * i, carry)
            body(2 * i + 1, carry)
            return carry

        lax.fori_loop(0, group // 2, pair, 0)

    def middle(t, carry):
        section_two(t, 3, SX - 3, section_one(t, 3, SX + 1))
        return carry

    def outer(t, carry):
        section_two(t, 0, 1, section_one(t, 0, 3))
        section_two(t, SX - 1, SX, section_one(t, SX + 1, SX + 4))
        return carry

    def lower(t, carry):
        section_two(t, 1, 3, {})
        return carry

    def upper(t, carry):
        section_two(t, SX - 3, SX - 1, {})
        return carry

    def pack(x):
        v = part[x]
        for t in range(n_tracer):
            sb[t, x * 8 : (x + 1) * 8, :] = pltpu.roll(v, (1 - TY * t) % NY, 0)[0:8]

    def to_owners(i, lo, hi):
        rows = pl.ds(lo * 8, (hi - lo) * 8)
        return [
            rcopy(
                sb.at[trs[k], rows],
                rb.at[k, rows],
                buoy_send.at[2 + i, k],
                buoy_recv.at[2 + i, k],
                0,
                trs[k],
            )
            for k in range(1, n_tracer)
        ]

    buoy = [
        to_owners(i, lo, hi)
        for i, (lo, hi) in enumerate(((3, SX - 3), (0, 1), (SX - 1, SX), (1, 3), (SX - 3, SX - 1)))
    ]
    in_pairs(middle)
    for x in range(3, SX - 3):
        pack(x)
    each(buoy[0], "start")()
    for ds in (1, -1):
        where_there(-ds, 0, each(flow_arrivals(ds), "wait_recv"))
    for i in range(0, 3):
        widen(i)
    for i in range(SX + 3, SX + 6):
        widen(i)
    for i in range(0, 3):
        faces_x(i)
    for i in range(SX + 2, SX + 5):
        faces_x(i)
    for i in range(0, 2):
        faces_yz(i)
    for i in range(SX + 2, SX + 4):
        faces_yz(i)

    in_pairs(outer)
    pack(0)
    pack(SX - 1)
    sides = {}
    for ds, rows, dst in ((1, pl.ds((SX - 1) * 8, 8), 0), (-1, pl.ds(0, 8), 1)):
        sides[ds] = [
            rcopy(
                sb.at[trs[k], rows],
                rx.at[dst, k],
                buoy_send.at[dst, k],
                buoy_recv.at[dst, k],
                ds,
                trs[k],
            )
            for k in range(n_tracer)
        ]
        where_there(ds, 0, each(sides[ds], "start"))
    each(buoy[1] + buoy[2], "start")()
    in_pairs(lower)
    for x in (1, 2):
        pack(x)
    each(buoy[3], "start")()
    in_pairs(upper)
    for x in (SX - 3, SX - 2):
        pack(x)
    each(buoy[4], "start")()
    arrive(third)
    leave(first + second + third)
    for j in range(CHUNKS):
        leave(bulks[j])
    for ds in (1, -1, 0):
        where_there(ds, 0, each(flows[ds], "wait_send"))
    for ds in (1, -1):
        where_there(ds, 0, each(sides[ds], "wait_send"))
    for ds in (1, -1):
        where_there(-ds, 0, each(sides[ds], "wait_recv"))
    each([c for row in buoy for c in row], "wait_recv")()

    buf = 0
    for yy in range(-1, TY + 1):
        g = sb[tr, pl.ds(yy + 1, SX, stride=8), :]
        for k in range(1, n_tracer):
            g = g + rb[k, pl.ds(yy + 1, SX, stride=8), :]
        if yy < 0 or yy >= TY:
            side = 0 if yy < 0 else 1
            for k, q in enumerate(YD[side]):
                if DIRS[q][2]:
                    yr[2, side, k] = yr[2, side, k] + (3.0 * WEIGHTS[q] * DIRS[q][2]) * g
        else:
            for q in range(19):
                if DIRS[q][2]:
                    post[buf, q, yy] = post[buf, q, yy] + (3.0 * WEIGHTS[q] * DIRS[q][2]) * g
    for side in range(2):
        g = rx[side, 0]
        for k in range(1, n_tracer):
            g = g + rx[side, k]
        g = pltpu.roll(g, 7, 0)
        for k, q in enumerate(XD[side]):
            if DIRS[q][2]:
                xr[2, side, k] = xr[2, side, k] + (3.0 * WEIGHTS[q] * DIRS[q][2]) * g

    for y in range(TY):
        f = stream(2, y)
        rho, u = moments(f)
        for q in range(19):
            fout[pl.ds(q * SX * TY + y, SX, stride=TY), :] = f[q]
        for a in range(3):
            vout[pl.ds(a * SX * TY + y, SX, stride=TY), :] = u[a] * fluid_v[y]

    each([c for row in buoy for c in row], "wait_send")()


def hand_over(pop_in, vel_in, tracer_in, pop_out, vel_out, tracer_out, sem):
    part = tracer_in.shape[0] // 4
    pairs = [(a.at[pl.ds(i * part, part)], b.at[pl.ds(i * part, part)])
             for a, b in ((tracer_in, tracer_out),) for i in range(4)]
    pairs += [(pop_in, pop_out), (vel_in, vel_out)]
    copies = [pltpu.make_async_copy(a, b, sem.at[i]) for i, (a, b) in enumerate(pairs)]
    for c in copies:
        c.start()
    for c in copies:
        c.wait()


def local(
    n_space,
    n_tracer,
    populations,
    solid_mask,
    tracers,
    decay_rates,
    buoyancy_coeffs,
    source_cells,
    source_rates,
):
    group = tracers.shape[0]
    rows = SX * TY
    smem = pltpu.SMEM
    hbm = pl.BlockSpec(memory_space=pl.ANY)
    vmem = pltpu.VMEM
    dma = pltpu.SemaphoreType.DMA
    out = pl.pallas_call(
        functools.partial(kernel, n_space, n_tracer),
        out_shape=(
            vmem((19 * rows, NZ), F32),
            vmem((3 * rows, NZ), F32),
            vmem(tracers.shape, F32),
        ),
        in_specs=[pl.BlockSpec(memory_space=pltpu.HBM)] * 7,
        out_specs=(pl.BlockSpec(memory_space=pltpu.VMEM),) * 3,
        scratch_shapes=[
            smem((group,), F32),
            smem((group,), F32),
            smem(source_cells.shape[::-1], jnp.int32),
            smem(source_rates.shape[::-1], F32),
            vmem((19 * rows, NZ), F32),
            vmem((rows, NZ), jnp.int32),
            vmem((TY, SX, NZ), F32),
            vmem((19, TY, SX, NZ), F32),
            vmem((2, 19, TY, SX, NZ), F32),
            vmem((3, 2, 6, 8, NZ), F32),
            vmem((3, 2, 6, 8, NZ), F32),
            vmem((3, 2, 6, 8, NZ), F32),
            vmem((3, 2, 6, 8, NZ), F32),
            vmem((3, 4, 2, 8, NZ), F32),
            vmem((3, 4, 2, 8, NZ), F32),
            vmem((SX * 4 * TY, NZ), F32),
            vmem((n_tracer, SX + 6, 4 * TY, NZ), jnp.bfloat16),
            vmem((4, SX + 6, NY, NZ), F32),
            vmem((2, SX + 5, NY, NZ), F32),
            vmem((2, SX + 4, NY, NZ), F32),
            vmem((2, SX + 4, NY, NZ), F32),
            vmem((group, SX + 8, NY, NZ), F32),
            vmem((2, group, 2, NY, NZ), jnp.bfloat16),
            vmem((2, group, 2, NY, NZ), jnp.bfloat16),
            vmem((group, SX + 6, NY, NZ), F32),
            vmem((group, SX + 6, NY, NZ), F32),
            vmem((group, SX + 4, NY, NZ), F32),
            vmem((group, SX + 4, NY, NZ), F32),
            vmem((group, SX + 4, NY, NZ), F32),
            vmem((group, SX + 4, NY, NZ), F32),
            vmem((group, SX + 4, NY, NZ), F32),
            vmem((group, SX + 4, NY, NZ), F32),
            vmem((group, SX + 4, NY, NZ), F32),
            vmem((SX, NY, NZ), F32),
            vmem((n_tracer, SX * 8, NZ), F32),
            vmem((n_tracer, SX * 8, NZ), F32),
            vmem((2, n_tracer, 8, NZ), F32),
            dma((7,)),
            dma((3, 8)),
            dma((3, 8)),
            dma((4, CHUNKS)),
            dma((4, CHUNKS)),
            dma((3, n_tracer)),
            dma((3, n_tracer)),
            dma((7, n_tracer)),
            dma((7, n_tracer)),
        ],
        compiler_params=pltpu.CompilerParams(
            collective_id=0, has_side_effects=True, vmem_limit_bytes=65400000
        ),
        name="plume",
    )(
        decay_rates,
        buoyancy_coeffs,
        source_cells.T,
        source_rates.T,
        populations.reshape(19 * rows, NZ),
        solid_mask.reshape(rows, NZ),
        tracers,
    )
    out = pl.pallas_call(
        hand_over,
        out_shape=tuple(jax.ShapeDtypeStruct(v.shape, v.dtype) for v in out),
        in_specs=[hbm] * 3,
        out_specs=(hbm,) * 3,
        scratch_shapes=[dma((6,))],
        compiler_params=pltpu.CompilerParams(vmem_limit_bytes=1024 * 1024),
        name="hand_over",
    )(*out)
    return (
        out[0].reshape(populations.shape),
        out[1].reshape((3,) + populations.shape[1:]),
        out[2],
    )


def solution(mesh):
    placed = (
        P(None, "space", "tracer", None),
        P("space", "tracer", None),
        P("tracer", "space", None, None),
        P("tracer"),
        P("tracer"),
        P("tracer", None),
        P("tracer", None),
    )
    return jax.shard_map(
        functools.partial(local, mesh.shape["space"], mesh.shape["tracer"]),
        mesh=mesh,
        in_specs=placed,
        out_specs=(
            P(None, "space", "tracer", None),
            P(None, "space", "tracer", None),
            P("tracer", "space", None, None),
        ),
        check_vma=False,
    )
```
